128 devices in a mesh: slab: 8 (over y, core), ray: 16 (over z, x).
Axes of the slice: x: 4, y: 4, z: 4, core: 2. Of those that a mesh axis runs over, the one named last changes fastest.
Arguments:
- intensity: float32 [8, 16, 256, 2048], P('slab', 'ray'), may hold values from 0.2 to 1
- angles: float32 [8, 16], replicated, may hold values from 0 to 3.14159
- volume: float32 [256, 64, 256], P('slab', 'ray'), may hold values from -3 to 3
- vol_list: int32 [64], replicated, may hold values from 0 to 63, as said below
Outputs:
- reconstruction: float32 [256, 64, 256], P('slab', 'ray')
- residual: float32 [8, 16, 256, 2048], P(None, 'ray', 'slab')
The draws below stay inside these ranges and needn't reach their ends.
Inputs may be any that keep to these rules, and one draw needn't show every extreme that they name: vol_list is a permutation of the patch ids that follows a Hilbert curve over the 8 x 8 grid of patches.
All inputs are finite; a program needn't handle non-finite values.
Results may differ from the reference program's by a relative error of at most 0.0003.
Values sent between devices are 32-bit elements; how exact they have to be, the bound alone decides.
A program may use at most 192 MiB of HBM per device.

```python
import jax
import jax.numpy as jnp
from jax import lax

NCOL = 2048
NSLICE = 256
BAND = 2048
HLEV = 3
TR = 32
ANG_RAY = 8
PGRID = 8
ROI = 128
PATCHES = 64
N_RAY = 16


def draw_intensity(key, part):
    key_list = jax.random.split(jax.random.fold_in(key, 23), 10)
    lead_shape = (ANG_RAY, N_RAY)
    mode_count = 6
    row_pos = jnp.arange(NSLICE, dtype=jnp.float32)[:, None] / NSLICE
    col_pos = jnp.arange(NCOL, dtype=jnp.float32)[None, :] / NCOL
    row_int = jnp.arange(NSLICE, dtype=jnp.int32)[:, None]
    col_int = jnp.arange(NCOL, dtype=jnp.int32)[None, :]
    offsets = 0.6 * jax.random.normal(key_list[0], lead_shape, jnp.float32)
    mode_scale = 0.6
    roughness = jax.random.uniform(key_list[1], lead_shape + (NSLICE, NCOL), jnp.float32, -0.8, 0.8)
    row_freq = jax.random.randint(key_list[2], lead_shape + (mode_count,), 0, 3).astype(jnp.float32)
    col_freq = jax.random.randint(key_list[3], lead_shape + (mode_count,), 0, 9).astype(jnp.float32)
    amplitude = mode_scale * jax.random.normal(key_list[4], lead_shape + (mode_count,), jnp.float32)
    phases = jax.random.uniform(key_list[5], lead_shape + (mode_count,), jnp.float32, -jnp.pi, jnp.pi)
    col_edges = jax.random.randint(key_list[6], lead_shape + (3,), 0, NCOL)
    col_steps = 0.8 * jax.random.normal(key_list[7], lead_shape + (3,), jnp.float32)
    row_edges = jax.random.randint(key_list[8], lead_shape, 0, NSLICE)
    row_steps = 0.8 * jax.random.normal(key_list[9], lead_shape, jnp.float32)
    field_sum = roughness + offsets[:, :, None, None]
    for mode_idx in range(mode_count):
        phase_map = 2.0 * jnp.pi * (row_freq[:, :, mode_idx, None, None] * row_pos + col_freq[:, :, mode_idx, None, None] * col_pos) + phases[:, :, mode_idx, None, None]
        field_sum = field_sum + amplitude[:, :, mode_idx, None, None] * jnp.cos(phase_map)
    for edge_idx in range(3):
        upper_part = (col_int >= col_edges[:, :, edge_idx, None, None]).astype(jnp.float32)
        field_sum = field_sum + col_steps[:, :, edge_idx, None, None] * upper_part
    lower_rows = (row_int >= row_edges[:, :, None, None]).astype(jnp.float32)
    field_sum = field_sum + row_steps[:, :, None, None] * lower_rows
    return 0.2 + 0.8 * jax.nn.sigmoid(field_sum)


def draw_vol_list(key, part):
    keys = jax.random.split(jax.random.fold_in(key, 11), 2)
    grid_side = 2 ** HLEV
    total = grid_side * grid_side
    shift = jax.random.randint(keys[0], (), 0, total)
    flips = jax.random.randint(keys[1], (3,), 0, 2)
    remain = (jnp.arange(total, dtype=jnp.int32) + shift) % total
    position_across = jnp.zeros((total,), jnp.int32)
    position_down = jnp.zeros((total,), jnp.int32)
    current_edge_length = 1
    for level_idx in range(HLEV):
        bit_x = remain // 2 % 2
        bit_y = (remain + bit_x) % 2
        rotated_flag = bit_y == 0
        reflect_flag = jnp.logical_and(rotated_flag, bit_x == 1)
        reflected_across = jnp.where(reflect_flag, current_edge_length - 1 - position_across, position_across)
        reflected_down = jnp.where(reflect_flag, current_edge_length - 1 - position_down, position_down)
        updated_across = jnp.where(rotated_flag, reflected_down, reflected_across)
        updated_down = jnp.where(rotated_flag, reflected_across, reflected_down)
        position_across = updated_across + current_edge_length * bit_x
        position_down = updated_down + current_edge_length * bit_y
        remain = remain // 4
        current_edge_length = current_edge_length * 2
    x_swap = jnp.where(flips[0] == 1, position_down, position_across)
    y_swap = jnp.where(flips[0] == 1, position_across, position_down)
    x_fin = jnp.where(flips[1] == 1, grid_side - 1 - x_swap, x_swap)
    y_fin = jnp.where(flips[2] == 1, grid_side - 1 - y_swap, y_swap)
    return (x_fin * grid_side + y_fin).astype(jnp.int32)


def shard_levels(stream_key, dims, cuts, least, top_value):
    gain = 1.0
    for dim, blocks in cuts:
        draws = jax.random.uniform(jax.random.fold_in(jax.random.fold_in(stream_key, 6), dim), (blocks,), jnp.float32, least / len(cuts), top_value / len(cuts))
        gain = gain * jnp.repeat(jnp.exp(draws), dims[dim] // blocks).reshape((-1,) + (1,) * (len(dims) - 1 - dim))
    return gain


def centred(own_key, shape, scale, bound, pieces=(), held_as=jnp.bfloat16):
    loudness = shard_levels(own_key, shape, pieces, -0.22, 0.18) if pieces else 1.0
    drawn = jax.random.normal(own_key, shape, jnp.float32) * scale * loudness
    return jnp.minimum(jnp.maximum(drawn, -bound), bound).astype(held_as)


def setup_inputs(seed: int = 0) -> dict:
    splits = jax.random.split(jax.random.key(seed), 5)
    return {
        "intensity": draw_intensity(jax.random.fold_in(splits[4], 71), 0),
        "angles": jnp.clip(jax.random.uniform(splits[1], (ANG_RAY, N_RAY), jnp.float32, 0.0, 3.14159), 0.0, 3.14159),
        "volume": centred(splits[2], (NSLICE, PATCHES, 256), 0.5, 3.0, ((0, 8), (1, 16)), jnp.float32),
        "vol_list": draw_vol_list(jax.random.fold_in(splits[4], 71), 0),
    }


paganin_strength = 10.0
relax = 1.8
row_floor = 0.25
highest = lax.Precision.HIGHEST


def paganin_gain(height, width_px):
    freq_rows = 2.0 - 2.0 * jnp.cos(2.0 * jnp.pi * jnp.arange(height).astype(jnp.float32) / height)
    freq_cols = 2.0 - 2.0 * jnp.cos(2.0 * jnp.pi * jnp.arange(width_px).astype(jnp.float32) / width_px)
    return 1.0 / (1.0 + paganin_strength * (freq_rows[:, None] + freq_cols[None, :]))


def ray_windows(patch_ids, theta):
    half_roi = (ROI - 1) / 2.0
    half_band = (BAND - 1) / 2.0
    centre_x = (patch_ids // PGRID).astype(jnp.float32) * 16.0 + 7.5 - half_roi
    centre_y = (patch_ids % PGRID).astype(jnp.float32) * 16.0 + 7.5 - half_roi
    centre = half_band + centre_x[:, None] * jnp.cos(theta)[None, :] + centre_y[:, None] * jnp.sin(theta)[None, :]
    starts = jnp.floor(centre).astype(jnp.int32) - 15
    return starts[:, :, None] + jnp.arange(TR).astype(jnp.int32)[None, None, :]


def patch_weights(patch_ids, theta_one):
    half_roi = (ROI - 1) / 2.0
    half_band = (BAND - 1) / 2.0
    ray_index = ray_windows(patch_ids, theta_one[None])[:, 0, :]
    voxels = jnp.arange(256).astype(jnp.int32)
    voxel_x = (patch_ids // PGRID).astype(jnp.float32)[:, None] * 16.0 + (voxels // 16).astype(jnp.float32)[None, :] - half_roi
    voxel_y = (patch_ids % PGRID).astype(jnp.float32)[:, None] * 16.0 + (voxels % 16).astype(jnp.float32)[None, :] - half_roi
    along = voxel_x * jnp.cos(theta_one) + voxel_y * jnp.sin(theta_one)
    distance = (ray_index.astype(jnp.float32) - half_band)[:, None, :] - along[:, :, None]
    weights = jnp.maximum(0.0, 1.0 - jnp.abs(distance)) / ROI
    return weights, ray_index


def reference(intensity, angles, volume, vol_list):
    gain_table = paganin_gain(NSLICE, NCOL)
    spectrum = jnp.fft.fft2(intensity)
    filtered = jnp.real(jnp.fft.ifft2(spectrum * gain_table))
    offset = (NCOL - BAND) // 2
    projected = -jnp.log(filtered[..., offset:offset + BAND])
    all_angles = angles.reshape(-1)
    sinogram = projected.reshape(ANG_RAY * N_RAY, NSLICE, BAND)
    step_size = relax * ROI / (ANG_RAY * N_RAY)

    def forward(current):
        def project_one(theta_one):
            weights, ray_index = patch_weights(vol_list, theta_one)
            contrib = jnp.einsum("smv,mvj->smj", current, weights, precision=highest)
            predicted = jnp.zeros((NSLICE, BAND), jnp.float32).at[:, ray_index].add(contrib)
            sums = jnp.zeros((BAND,), jnp.float32).at[ray_index].add(jnp.sum(weights, axis=1))
            return predicted, sums
        return lax.map(project_one, all_angles)

    def backward(scaled):
        def accumulate(total, member):
            theta_one, sino_one = member
            weights, ray_index = patch_weights(vol_list, theta_one)
            windows = sino_one[:, ray_index]
            return total + jnp.einsum("smj,mvj->smv", windows, weights, precision=highest), None
        total, _ = lax.scan(accumulate, jnp.zeros(volume.shape, jnp.float32), (all_angles, scaled))
        return total

    predicted, row_sums = forward(volume)
    row_weight = 1.0 / jnp.maximum(row_sums, row_floor)
    difference = sinogram - predicted
    first_iterate = volume + step_size * backward(difference * row_weight[:, None, :])
    predicted_next, _ = forward(first_iterate)
    residual = sinogram - predicted_next
    reconstruction = first_iterate + step_size * backward(residual * row_weight[:, None, :])
    return reconstruction, residual.reshape(ANG_RAY, N_RAY, NSLICE, BAND)
```

```python
import functools

import jax
import jax.numpy as jnp
import numpy as np
from jax import lax
from jax.experimental import pallas as pl
from jax.experimental.pallas import tpu as pltpu
from jax.sharding import PartitionSpec as P

BAND = 2048
PGRID = 8
ROI = 128
HALF_ROI = (ROI - 1) / 2.0
HALF_BAND = (BAND - 1) / 2.0
STRENGTH = 10.0
RELAX = 1.8
ROW_FLOOR = 0.25
MESH = pl.DeviceIdType.MESH

TR = 32
MID0 = 896
MID = 256
RAY0 = 928
RAYS = 192
SKIP = RAY0 - MID0
STRIDE = RAYS
LEAD = RAYS - TR
F32 = jnp.float32
BF16 = jnp.bfloat16


def dot(a, b):
    return lax.dot_general(a, b, (((1,), (0,)), ((), ())), preferred_element_type=F32)


def dot_nt(a, b):
    return lax.dot_general(a, b, (((1,), (1,)), ((), ())), preferred_element_type=F32)


def split(v):
    hi = v.astype(BF16)
    return hi, (v - hi.astype(F32)).astype(BF16)


def filter_tables(height, width):
    m = np.arange(height)
    ang = 2.0 * np.pi * (np.outer(m, m) % height) / height
    had = (np.cos(ang) + np.sin(ang)) / np.sqrt(height)
    hi = had.astype(jnp.bfloat16)
    lo = (had - hi.astype(np.float64)).astype(jnp.bfloat16)
    beta = 1.0 + STRENGTH * (2.0 - 2.0 * np.cos(2.0 * np.pi * m / height)) + 2.0 * STRENGTH
    half = beta / (2.0 * STRENGTH)
    root = half - np.sqrt(half * half - 1.0)
    scale = root / STRENGTH / (1.0 - root**width) ** 2
    wide = np.ones((1, 128))
    return (
        hi,
        lo,
        (root[:, None] * wide).astype(np.float32),
        (scale[:, None] * wide).astype(np.float32),
    )


def filter_kernel(img, hi_ref, lo_ref, root_ref, scale_ref, out, mid):
    height, width = img.shape
    chunk = 512
    h_hi = hi_ref[...]
    h_lo = lo_ref[...]

    def apply(v):
        v_hi, v_lo = split(v)
        return dot(h_hi, v_hi) + (dot(h_hi, v_lo) + dot(h_lo, v_hi))

    @pl.loop(0, width // chunk)
    def _(c):
        cols = pl.ds(pl.multiple_of(c * chunk, chunk), chunk)
        mid[:, cols] = apply(1.0 - img[:, cols])

    @pl.loop(0, height // 8)
    def _(g):
        rows = pl.ds(pl.multiple_of(g * 8, 8), 8)
        root = root_ref[rows, :]
        v = mid[rows, :]
        for back in (False, True):
            power = root
            step = 1
            while step < width:
                wide = jnp.concatenate([power] * (width // 128), axis=1)
                v = v + wide * pltpu.roll(v, width - step if back else step, 1)
                power = power * power
                step *= 2
        mid[rows, :] = v * jnp.concatenate([scale_ref[rows, :]] * (width // 128), axis=1)

    @pl.loop(0, width // chunk)
    def _(c):
        cols = pl.ds(pl.multiple_of(c * chunk, chunk), chunk)
        out[:, cols] = -jnp.log(1.0 - apply(mid[:, cols]))


def paganin(images):
    height, width = images.shape
    tables = filter_tables(height, width)
    return pl.pallas_call(
        filter_kernel,
        out_shape=jax.ShapeDtypeStruct(images.shape, F32),
        in_specs=[pl.BlockSpec(memory_space=pltpu.VMEM)] * 5,
        out_specs=pl.BlockSpec(memory_space=pltpu.VMEM),
        scratch_shapes=[pltpu.VMEM((height, width), F32)],
        compiler_params=pltpu.CompilerParams(vmem_limit_bytes=40 << 20),
        name="paganin_filter",
    )(images, *[jnp.asarray(t) for t in tables])


def sirt_kernel(
    dims,
    starts,
    offs,
    cs,
    ysend,
    x0,
    res,
    rec,
    w_hi,
    w_lo,
    xb,
    pad,
    xg,
    xh,
    zs0,
    zr0,
    zs1,
    zr1,
    dg,
    dh,
    dr,
    tile,
    th,
    tl,
    pv0,
    pr0,
    pv1,
    pr1,
    ymid,
    yt,
    weight,
    yown,
    rmid,
    s_mid,
    r_mid,
    s_left,
    r_left,
    s_right,
    r_right,
    s_x,
    r_x,
    s_z,
    r_z,
    s_loc,
):
    ns, nz, nx = dims
    slots = 4
    np_group = slots * nx
    na = ns * nz
    quads = ns // 4
    right0 = MID0 + MID
    rightn = BAND - right0
    slab = lax.axis_index("slab")
    ray = lax.axis_index("ray")
    z = ray // nx
    x = lax.rem(ray, nx)

    def at_slab(t):
        return {"slab": lax.rem(slab + t, ns), "ray": ray}

    def at_z(t):
        return {"slab": slab, "ray": lax.rem(z + t, nz) * nx + x}

    def at_x(t):
        return {"slab": slab, "ray": z * nx + lax.rem(x + t, nx)}

    barrier = pltpu.get_barrier_semaphore()
    for t in range(1, nx):
        pl.semaphore_signal(barrier, inc=1, device_id=at_x(t), device_id_type=MESH)
    for t in range(1, nz):
        pl.semaphore_signal(barrier, inc=1, device_id=at_z(t), device_id_type=MESH)
    for t in range(1, ns):
        pl.semaphore_signal(barrier, inc=1, device_id=at_slab(t), device_id_type=MESH)
    pl.semaphore_wait(barrier, nx + nz + ns - 3)

    def send(src, dst, ssem, rsem, device):
        return pltpu.make_async_remote_copy(
            src_ref=src, dst_ref=dst, send_sem=ssem, recv_sem=rsem, device_id=device, device_id_type=MESH
        )

    x_out = [
        send(x0, xg.at[x], s_x.at[0, t - 1], r_x.at[0, t - 1], at_x(t)) for t in range(1, nx)
    ]
    for c in x_out:
        c.start()
    y_mid, y_side = [], []
    for t in range(1, ns):
        to = lax.rem(slab + t, ns)
        y_mid.append(
            send(
                ysend.at[to, :, pl.ds(MID0, MID)], ymid.at[slab], s_mid.at[t - 1], r_mid.at[t - 1], at_slab(t)
            )
        )
        y_side.append(
            send(
                ysend.at[to, :, pl.ds(0, MID0)],
                res.at[slab, :, pl.ds(0, MID0)],
                s_left.at[t - 1],
                r_left.at[t - 1],
                at_slab(t),
            )
        )
        y_side.append(
            send(
                ysend.at[to, :, pl.ds(right0, rightn)],
                res.at[slab, :, pl.ds(right0, rightn)],
                s_right.at[t - 1],
                r_right.at[t - 1],
                at_slab(t),
            )
        )
    for c in y_mid + y_side:
        c.start()
    own_in = pltpu.make_async_copy(ysend.at[slab], yown, s_loc.at[0])
    own_in.start()

    vox = lax.broadcasted_iota(jnp.int32, (1, 256), 1)
    dx = (vox // 16).astype(F32) - 7.5
    dy = lax.rem(vox, 16).astype(F32) - 7.5
    lane_ray = lax.broadcasted_iota(jnp.int32, (TR, 256), 0).astype(F32)

    @pl.loop(0, na)
    def _(a):
        base = lane_ray - (dx * cs[a] + dy * cs[na + a])
        rows = pl.ds(pl.multiple_of(a * TR, TR), TR)

        @pl.loop(0, np_group)
        def _(p):
            hat = jnp.maximum(0.0, 1.0 - jnp.abs(base + offs[p * na + a]))
            hi, lo = split(hat)
            w_hi[p, rows, :] = hi
            w_lo[p, rows, :] = lo

    @pl.loop(0, ns)
    def _(a):
        for p in range(np_group):
            pad[a, pl.ds(p * STRIDE // 8, LEAD // 8)] = jnp.zeros((LEAD // 8, 8, 128), F32)
        pad[a, pl.ds(np_group * STRIDE // 8, LEAD // 8)] = jnp.zeros((LEAD // 8, 8, 128), F32)

    @pl.loop(0, np_group)
    def _(p):
        xb[p, 64:96, :] = jnp.ones((32, 256), BF16)
        xb[p, 96:128, :] = jnp.zeros((32, 256), BF16)

    lane = lax.broadcasted_iota(jnp.int32, (1, 128), 1) // 32

    def load_volume(source):
        for q in range(nx):
            for s in range(slots):
                hi, lo = split(source[q, :, pl.ds(s * 256, 256)])
                xb[q * slots + s, 0:32, :] = hi
                xb[q * slots + s, 32:64, :] = lo

    def forward(zs, zr, phase):
        with_sums = phase == 0

        @pl.loop(0, nz)
        def _(t):
            o = lax.rem(z + 1 + t, nz)
            rows = pl.ds(pl.multiple_of(o * (ns * TR), ns * TR), ns * TR)

            @pl.loop(0, np_group)
            def _(p):
                part = dot_nt(w_hi[p, rows, :], xb[p]) + dot_nt(w_lo[p, rows, :], xb[p])
                at = pl.ds(p * (STRIDE // 8) + LEAD // 8, TR // 8)
                for a in range(ns):
                    pad[a, at] = part[a * TR : (a + 1) * TR].reshape(TR // 8, 8, 128)

            @pl.loop(0, quads)
            def _(g):
                packed = jnp.zeros((RAYS, 128), F32)
                sums = jnp.zeros((RAYS, 128), F32)
                for i in range(4):
                    a = g * 4 + i
                    acc = jnp.zeros((RAYS, 128), F32)
                    for p in range(np_group):
                        first = (p * STRIDE + LEAD) // 8 - starts[p * na + o * ns + a]
                        acc = acc + pad[a, pl.ds(first, RAYS // 8)].reshape(RAYS, 128)
                    both = acc + pltpu.roll(acc, 96, 1)
                    packed = jnp.where(lane == i, pltpu.roll(both, 32 * i, 1) if i else both, packed)
                    if with_sums:
                        sums = jnp.where(
                            lane == i, pltpu.roll(acc, (64 + 32 * i) % 128, 1) if i != 2 else acc, sums
                        )
                zs[t, g] = packed
                if with_sums:
                    zs[t, quads + g] = sums

            @pl.when(t < nz - 1)
            def _():
                send(zs.at[t], zr.at[t], s_z.at[phase, t], r_z.at[phase, t], at_z(1 + t)).start()

    def end_forward(zs, zr, phase):
        for t in range(nz - 1):
            c = send(zs.at[t], zr.at[t], s_z.at[phase, t], r_z.at[phase, t], at_z(1 + t))
            c.wait_send()
            c.wait_recv()

    def total_rays(zs, zr, index):
        v = zs[nz - 1, index]
        for t in range(nz - 1):
            v = v + zr[t, index]
        return v * (1.0 / ROI)

    def spread(buf, phase):
        out = [
            send(buf.at[z], buf.at[z], s_z.at[phase, t - 1], r_z.at[phase, t - 1], at_z(t))
            for t in range(1, nz)
        ]
        for c in out:
            c.start()
        return out

    def backward(buf, pv, pr, phase):
        @pl.loop(0, nz)
        def _(o):
            for g in range(quads):
                v = buf[o, g]
                for i in range(4):
                    m = jnp.where(lane == i, v, 0.0)
                    m = m + pltpu.roll(m, 32, 1)
                    m = m + pltpu.roll(m, 64, 1)
                    dr[o * ns + g * 4 + i] = m.reshape(RAYS // 8, 8, 128)

        @pl.loop(0, nx)
        def _(t):
            q = lax.rem(x + 1 + t, nx)

            @pl.loop(0, na // 4)
            def _(b):
                for j in range(4):
                    a = b * 4 + j
                    out = None
                    for s in range(slots):
                        first = starts[(q * slots + s) * na + a]
                        v = dr[a, pl.ds(first, TR // 8)].reshape(TR, 128)
                        out = v if s == 0 else jnp.where(lane == s, v, out)
                    tile[j * TR : (j + 1) * TR, :] = out
                hi, lo = split(jnp.transpose(tile[...]))
                cols = pl.ds(pl.multiple_of(b * 128, 128), 128)
                th[:, cols] = hi
                tl[:, cols] = lo

            for s in range(slots):
                p = q * slots + s
                hi = th[s * 32 : (s + 1) * 32, :]
                lo = tl[s * 32 : (s + 1) * 32, :]
                pv[t, :, s * 256 : (s + 1) * 256] = dot(hi, w_hi[p]) + (dot(lo, w_hi[p]) + dot(hi, w_lo[p]))

            @pl.when(t < nx - 1)
            def _():
                send(pv.at[t], pr.at[t], s_x.at[phase, t], r_x.at[phase, t], at_x(1 + t)).start()

        for t in range(nx - 1):
            c = send(pv.at[t], pr.at[t], s_x.at[phase, t], r_x.at[phase, t], at_x(1 + t))
            c.wait_send()
            c.wait_recv()
        v = pv[nx - 1]
        for t in range(nx - 1):
            v = v + pr[t]
        return v * (RELAX / (ns * nz * nx))

    xg[x] = x0[...]
    for c in x_out:
        c.wait()
    load_volume(xg)
    forward(zs0, zr0, 0)

    own_in.wait()
    ymid[slab] = yown[:, MID0 : MID0 + MID]
    own_out = [
        pltpu.make_async_copy(yown.at[:, pl.ds(0, MID0)], res.at[slab, :, pl.ds(0, MID0)], s_loc.at[1]),
        pltpu.make_async_copy(
            yown.at[:, pl.ds(right0, rightn)], res.at[slab, :, pl.ds(right0, rightn)], s_loc.at[2]
        ),
    ]
    for c in own_out:
        c.start()
    for c in y_mid:
        c.wait()
    for g in range(quads):
        block = ymid[g * 4 : (g + 1) * 4].reshape(128, MID)
        for h in range(MID // 128):
            yt[g, h * 128 : (h + 1) * 128, :] = jnp.transpose(block[:, h * 128 : (h + 1) * 128])
    end_forward(zs0, zr0, 0)
    for g in range(quads):
        weight[g] = 1.0 / jnp.maximum(total_rays(zs0, zr0, quads + g), ROW_FLOOR)
        dg[z, g] = (yt[g, SKIP : SKIP + RAYS, :] - total_rays(zs0, zr0, g)) * weight[g]
    d_out = spread(dg, 1)
    for c in d_out:
        c.wait()
    first = x0[...] + backward(dg, pv0, pr0, 1)
    xh[x] = first
    x_out = [
        send(xh.at[x], xh.at[x], s_x.at[2, t - 1], r_x.at[2, t - 1], at_x(t)) for t in range(1, nx)
    ]
    for c in x_out:
        c.start()
    for c in x_out:
        c.wait()
    load_volume(xh)
    forward(zs1, zr1, 2)
    end_forward(zs1, zr1, 2)
    for g in range(quads):
        diff = yt[g, SKIP : SKIP + RAYS, :] - total_rays(zs1, zr1, g)
        dh[z, g] = diff * weight[g]
        yt[g, SKIP : SKIP + RAYS, :] = diff
    d_out = spread(dh, 3)
    for g in range(quads):
        for h in range(MID // 128):
            turned = jnp.transpose(yt[g, h * 128 : (h + 1) * 128, :])
            rmid[g * 4 : (g + 1) * 4, :, h * 128 : (h + 1) * 128] = turned.reshape(4, 32, 128)
    mid_out = pltpu.make_async_copy(rmid, res.at[:, :, pl.ds(MID0, MID)], s_loc.at[3])
    mid_out.start()
    for c in d_out:
        c.wait()
    rec[...] = first + backward(dh, pv1, pr1, 3)

    mid_out.wait()
    for c in own_out + y_side:
        c.wait()


def sirt(starts, offs, cs, ysend, x0, dims):
    ns, nz, nx = dims
    np_group = 4 * nx
    na = ns * nz
    rows = na * TR
    quads = ns // 4
    dma = pltpu.SemaphoreType.DMA
    vm = pltpu.VMEM
    smem = pl.BlockSpec(memory_space=pltpu.SMEM)
    peers_z = max(nz - 1, 1)
    peers_x = max(nx - 1, 1)
    return pl.pallas_call(
        functools.partial(sirt_kernel, dims),
        out_shape=(
            jax.ShapeDtypeStruct((ns, 32, BAND), F32),
            jax.ShapeDtypeStruct((32, 1024), F32),
        ),
        in_specs=[smem, smem, smem, pl.BlockSpec(memory_space=pl.ANY), pl.BlockSpec(memory_space=pltpu.VMEM)],
        out_specs=(pl.BlockSpec(memory_space=pl.ANY), pl.BlockSpec(memory_space=pltpu.VMEM)),
        scratch_shapes=[
            vm((np_group, rows, 256), BF16),
            vm((np_group, rows, 256), BF16),
            vm((np_group, 128, 256), BF16),
            vm((ns, (np_group * STRIDE + LEAD) // 8, 8, 128), F32),
            vm((nx, 32, 1024), F32),
            vm((nx, 32, 1024), F32),
            vm((nz, 2 * quads, RAYS, 128), F32),
            vm((peers_z, 2 * quads, RAYS, 128), F32),
            vm((nz, quads, RAYS, 128), F32),
            vm((peers_z, quads, RAYS, 128), F32),
            vm((nz, quads, RAYS, 128), F32),
            vm((nz, quads, RAYS, 128), F32),
            vm((na, RAYS // 8, 8, 128), F32),
            vm((128, 128), F32),
            vm((128, rows), BF16),
            vm((128, rows), BF16),
            vm((nx, 32, 1024), F32),
            vm((peers_x, 32, 1024), F32),
            vm((nx, 32, 1024), F32),
            vm((peers_x, 32, 1024), F32),
            vm((ns, 32, MID), F32),
            vm((quads, MID, 128), F32),
            vm((quads, RAYS, 128), F32),
            vm((32, BAND), F32),
            vm((ns, 32, MID), F32),
            dma((ns - 1,)),
            dma((ns - 1,)),
            dma((ns - 1,)),
            dma((ns - 1,)),
            dma((ns - 1,)),
            dma((ns - 1,)),
            dma((4, peers_x)),
            dma((4, peers_x)),
            dma((4, peers_z)),
            dma((4, peers_z)),
            dma((4,)),
        ],
        compiler_params=pltpu.CompilerParams(
            collective_id=0, has_side_effects=True, vmem_limit_bytes=62 << 20
        ),
        name="sirt",
    )(starts, offs, cs, ysend, x0)


def tile_tables(angles, vol_list, z, x, nz, nx):
    theta = lax.dynamic_index_in_dim(angles.reshape(-1, nz, nx), x, 2, keepdims=False)
    theta = jnp.transpose(theta).reshape(-1)
    ids = lax.dynamic_slice_in_dim(vol_list, z * 4 * nx, 4 * nx)
    cosine = jnp.cos(theta)
    sine = jnp.sin(theta)
    centre_x = (ids // PGRID).astype(F32) * 16.0 + 7.5 - HALF_ROI
    centre_y = (ids % PGRID).astype(F32) * 16.0 + 7.5 - HALF_ROI
    centre = HALF_BAND + centre_x[:, None] * cosine[None, :] + centre_y[:, None] * sine[None, :]
    first = jnp.floor(centre - 11.61).astype(jnp.int32) + 1
    start = first // 8
    offs = (start * 8).astype(F32) - centre
    return (start - RAY0 // 8).reshape(-1), offs.reshape(-1), jnp.concatenate([cosine, sine])


def local(dims, intensity, angles, volume, vol_list):
    ns, nz, nx = dims
    rank = lax.axis_index("ray")
    height = intensity.shape[2]
    sino = paganin(intensity.reshape(height, BAND))
    starts, offs, cs = tile_tables(angles, vol_list, rank // nx, rank % nx, nz, nx)
    res, rec = sirt(starts, offs, cs, sino.reshape(ns, height // ns, BAND), volume.reshape(32, 1024), dims)
    return rec.reshape(volume.shape), res[:, None]


def make(mesh, dims):
    placed = (P("slab", "ray", None, None), P(), P("slab", "ray", None), P())
    return jax.shard_map(
        functools.partial(local, dims),
        mesh=mesh,
        in_specs=placed,
        out_specs=(P("slab", "ray", None), P(None, "ray", "slab", None)),
        check_vma=False,
    )


def solution(mesh):
    return make(mesh, (mesh.shape["slab"], 4, mesh.shape["ray"] // 4))
```

```python
import functools

import jax
import jax.numpy as jnp
import numpy as np
from jax import lax
from jax.experimental import pallas as pl
from jax.experimental.pallas import tpu as pltpu
from jax.sharding import PartitionSpec as P

BAND = 2048
PGRID = 8
ROI = 128
HALF_ROI = (ROI - 1) / 2.0
HALF_BAND = (BAND - 1) / 2.0
STRENGTH = 10.0
RELAX = 1.8
ROW_FLOOR = 0.25
MESH = pl.DeviceIdType.MESH

TR = 32
MID0 = 896
MID = 256
RAY0 = 928
RAYS = 192
SKIP = RAY0 - MID0
STRIDE = RAYS
LEAD = RAYS - TR
F32 = jnp.float32
BF16 = jnp.bfloat16
HALO = 64


def dot(a, b):
    return lax.dot_general(a, b, (((1,), (0,)), ((), ())), preferred_element_type=F32)


def dot_nt(a, b):
    return lax.dot_general(a, b, (((1,), (1,)), ((), ())), preferred_element_type=F32)


def split(v):
    hi = v.astype(BF16)
    return hi, (v - hi.astype(F32)).astype(BF16)


def filter_tables(height, width):
    m = np.arange(height)
    ang = 2.0 * np.pi * (np.outer(m, m) % height) / height
    had = (np.cos(ang) + np.sin(ang)) / np.sqrt(height)
    hi = had.astype(jnp.bfloat16)
    lo = (had - hi.astype(np.float64)).astype(jnp.bfloat16)
    beta = 1.0 + STRENGTH * (2.0 - 2.0 * np.cos(2.0 * np.pi * m / height)) + 2.0 * STRENGTH
    half = beta / (2.0 * STRENGTH)
    root = half - np.sqrt(half * half - 1.0)
    scale = root / STRENGTH / (1.0 - root**width) ** 2
    steps = int(np.log2(width))
    table = np.zeros((16, height))
    power = root
    for k in range(steps):
        table[k] = power / (1.0 + power * power)
        scale = scale * (1.0 + power * power)
        power = power * power
    table[15] = scale
    return hi, lo, table.astype(np.float32)


def filter_forward(img, h_hi, h_lo, table, ping, pong):
    height, width = img.shape
    chunk = 256
    halves = height // 128

    @pl.loop(0, width // chunk)
    def _(c):
        cols = pl.ds(pl.multiple_of(c * chunk, chunk), chunk)
        rows = pl.ds(pl.multiple_of(HALO + c * chunk, 8), chunk)
        v_hi, v_lo = split(jnp.transpose(1.0 - img[:, cols]))
        v = dot(v_hi, h_hi[...]) + (dot(v_lo, h_hi[...]) + dot(v_hi, h_lo[...]))
        for h in range(halves):
            ping[h, rows, :] = v[:, h * 128 : (h + 1) * 128]

    def row(k, h):
        return jnp.broadcast_to(table[k : k + 1, h * 128 : (h + 1) * 128], (8, 128))

    source, target = ping, pong
    step, k = 1, 0
    while step <= HALO:
        for h in range(halves):
            source[h, 0:HALO, :] = source[h, width : width + HALO, :]
            source[h, width + HALO : width + 2 * HALO, :] = source[h, HALO : 2 * HALO, :]
            rate = row(k, h)

            @pl.loop(0, width // 128)
            def _(b, h=h, step=step, source=source, target=target, rate=rate):
                for i in range(16):
                    at = b * 128 + HALO + 8 * i
                    here = source[h, pl.ds(at, 8), :]
                    near = source[h, pl.ds(at - step, 8), :] + source[h, pl.ds(at + step, 8), :]
                    target[h, pl.ds(at, 8), :] = here + rate * near

        source, target = target, source
        step *= 2
        k += 1

    for h in range(halves):
        rates = [row(j, h) for j in range(k, k + 4)]
        scale = row(15, h)

        @pl.loop(0, 16)
        def _(i, h=h, rates=rates, scale=scale):
            v = [source[h, pl.ds(HALO + b * 128 + 8 * i, 8), :] for b in range(16)]
            for j, rate in zip((1, 2, 4, 8), rates):
                v = [v[b] + rate * (v[b - j] + v[(b + j) % 16]) for b in range(16)]
            for b in range(16):
                target[h, pl.ds(HALO + b * 128 + 8 * i, 8), :] = v[b] * scale

    return target


def filter_back(modes, h_hi, h_lo, out, first, count):
    rows = pl.ds(HALO + first, count)
    v = jnp.concatenate([modes[h, rows, :] for h in range(out.shape[0] // 128)], axis=1)
    v_hi, v_lo = split(v)
    v = dot_nt(h_hi[...], v_hi) + (dot_nt(h_hi[...], v_lo) + dot_nt(h_lo[...], v_hi))
    out[:, pl.ds(first, count)] = -jnp.log(1.0 - v)


def sirt_kernel(
    dims,
    starts,
    offs,
    cs,
    image,
    h_hi_in,
    h_lo_in,
    table_in,
    x0,
    res,
    rec,
    img,
    ping,
    pong,
    h_hi,
    h_lo,
    table,
    parts_hi,
    parts_lo,
    pick,
    sums_pick,
    copy_out,
    copy_sum,
    w_hi,
    w_lo,
    xb,
    pad,
    xg,
    xh,
    zs0,
    zr0,
    zs1,
    zr1,
    dg,
    dh,
    dr,
    tile,
    th,
    pv0,
    pr0,
    pv1,
    pr1,
    ymid,
    yt,
    weight,
    rmid,
    s_mid,
    r_mid,
    s_left,
    r_left,
    s_right,
    r_right,
    s_x,
    r_x,
    s_z,
    r_z,
    s_loc,
):
    ns, nz, nx = dims
    slots = 4
    np_group = slots * nx
    na = ns * nz
    quads = ns // 4
    right0 = MID0 + MID
    rightn = BAND - right0
    slab = lax.axis_index("slab")
    ray = lax.axis_index("ray")
    z = ray // nx
    x = lax.rem(ray, nx)

    def at_slab(t):
        return {"slab": lax.rem(slab + t, ns), "ray": ray}

    def at_z(t):
        return {"slab": slab, "ray": lax.rem(z + t, nz) * nx + x}

    def at_x(t):
        return {"slab": slab, "ray": z * nx + lax.rem(x + t, nx)}

    loads = [
        pltpu.make_async_copy(image, img, s_loc.at[0]),
        pltpu.make_async_copy(h_hi_in, h_hi, s_loc.at[4]),
        pltpu.make_async_copy(h_lo_in, h_lo, s_loc.at[5]),
        pltpu.make_async_copy(table_in, table, s_loc.at[6]),
    ]
    for c in loads:
        c.start()
    barrier = pltpu.get_barrier_semaphore()
    for t in range(1, nx):
        pl.semaphore_signal(barrier, inc=1, device_id=at_x(t), device_id_type=MESH)
    for t in range(1, nz):
        pl.semaphore_signal(barrier, inc=1, device_id=at_z(t), device_id_type=MESH)
    for t in range(1, ns):
        pl.semaphore_signal(barrier, inc=1, device_id=at_slab(t), device_id_type=MESH)
    pl.semaphore_wait(barrier, nx + nz + ns - 3)

    def send(src, dst, ssem, rsem, device):
        return pltpu.make_async_remote_copy(
            src_ref=src, dst_ref=dst, send_sem=ssem, recv_sem=rsem, device_id=device, device_id_type=MESH
        )

    x_out = [
        send(x0, xg.at[x], s_x.at[0, t - 1], r_x.at[0, t - 1], at_x(t)) for t in range(1, nx)
    ]
    for c in x_out:
        c.start()
    y_mid, y_side = [], []
    own_rows = pl.ds(pl.multiple_of(slab * 32, 32), 32)
    for t in range(1, ns):
        to = pl.ds(pl.multiple_of(lax.rem(slab + t, ns) * 32, 32), 32)
        y_mid.append(
            send(
                img.at[to, pl.ds(MID0, MID)], ymid.at[slab], s_mid.at[t - 1], r_mid.at[t - 1], at_slab(t)
            )
        )
        y_side.append(
            send(
                img.at[to, pl.ds(0, MID0)],
                res.at[slab, :, pl.ds(0, MID0)],
                s_left.at[t - 1],
                r_left.at[t - 1],
                at_slab(t),
            )
        )
        y_side.append(
            send(
                img.at[to, pl.ds(right0, rightn)],
                res.at[slab, :, pl.ds(right0, rightn)],
                s_right.at[t - 1],
                r_right.at[t - 1],
                at_slab(t),
            )
        )

    vox = lax.broadcasted_iota(jnp.int32, (1, 256), 1)
    dx = (vox // 16).astype(F32) - 7.5
    dy = lax.rem(vox, 16).astype(F32) - 7.5
    lane_ray = lax.broadcasted_iota(jnp.int32, (TR, 256), 0).astype(F32)

    @pl.loop(0, na)
    def _(a):
        base = lane_ray - (dx * cs[a] + dy * cs[na + a])
        rows = pl.ds(pl.multiple_of(a * TR, TR), TR)

        @pl.loop(0, np_group)
        def _(p):
            hat = jnp.maximum(0.0, 1.0 - jnp.abs(base + offs[p * na + a]))
            hi, lo = split(hat)
            w_hi[p, rows, :] = hi
            w_lo[p, rows, :] = lo

    @pl.loop(0, ns)
    def _(a):
        for p in range(np_group):
            pad[a, pl.ds(p * STRIDE // 8, LEAD // 8)] = jnp.zeros((LEAD // 8, 8, 128), F32)
        pad[a, pl.ds(np_group * STRIDE // 8, LEAD // 8)] = jnp.zeros((LEAD // 8, 8, 128), F32)

    @pl.loop(0, np_group)
    def _(p):
        xb[p, 64:96, :] = jnp.ones((32, 256), BF16)
        xb[p, 96:128, :] = jnp.zeros((32, 256), BF16)

    lane = lax.broadcasted_iota(jnp.int32, (1, 128), 1) // 32

    def one_hot(shape, test):
        r = lax.broadcasted_iota(jnp.int32, shape, 0)
        c = lax.broadcasted_iota(jnp.int32, shape, 1)
        return jnp.where(test(r, c), 1.0, 0.0).astype(BF16)

    pick[...] = one_hot(
        (512, 128), lambda r, c: (r % 128 < 64) & (r % 32 == c % 32) & (r // 128 == c // 32)
    )
    for g in range(quads):
        sums_pick[g] = one_hot((512, 128), lambda r, c, g=g: (r % 128 == 64) & (g * 4 + r // 128 == c // 16))
        copy_sum[g] = one_hot((128, 128), lambda r, c, g=g: r == (g * 4 + c // 32) * 16)
    copy_out[...] = one_hot((128, 512), lambda r, c: (r // 32 == c // 128) & (r % 32 == c % 32))

    def load_volume(source):
        for q in range(nx):
            for s in range(slots):
                hi, lo = split(source[q, :, pl.ds(s * 256, 256)])
                xb[q * slots + s, 0:32, :] = hi
                xb[q * slots + s, 32:64, :] = lo

    def forward(zs, zr, phase):
        with_sums = phase == 0

        @pl.loop(0, nz)
        def _(t):
            o = lax.rem(z + 1 + t, nz)
            rows = pl.ds(pl.multiple_of(o * (ns * TR), ns * TR), ns * TR)

            @pl.loop(0, np_group, unroll=8)
            def _(p):
                part = dot_nt(w_hi[p, rows, :], xb[p]) + dot_nt(w_lo[p, rows, :], xb[p])
                at = pl.ds(p * (STRIDE // 8) + LEAD // 8, TR // 8)
                for a in range(ns):
                    pad[a, at] = part[a * TR : (a + 1) * TR].reshape(TR // 8, 8, 128)

            @pl.loop(0, quads)
            def _(g):
                for i in range(4):
                    a = g * 4 + i
                    acc = jnp.zeros((RAYS, 128), F32)
                    for p in range(np_group):
                        first = (p * STRIDE + LEAD) // 8 - starts[p * na + o * ns + a]
                        acc = acc + pad[a, pl.ds(first, RAYS // 8)].reshape(RAYS, 128)
                    hi, lo = split(acc)
                    parts_hi[:, i * 128 : (i + 1) * 128] = hi
                    parts_lo[:, i * 128 : (i + 1) * 128] = lo
                zs[t, g] = dot(parts_hi[...], pick[...]) + dot(parts_lo[...], pick[...])
                if with_sums:
                    part = dot(parts_hi[...], sums_pick[g]) + dot(parts_lo[...], sums_pick[g])
                    zs[t, quads] = jnp.where(g == 0, part, part + zs[t, quads])

            @pl.when(t < nz - 1)
            def _():
                send(zs.at[t], zr.at[t], s_z.at[phase, t], r_z.at[phase, t], at_z(1 + t)).start()

    def end_forward(zs, zr, phase):
        for t in range(nz - 1):
            c = send(zs.at[t], zr.at[t], s_z.at[phase, t], r_z.at[phase, t], at_z(1 + t))
            c.wait_send()
            c.wait_recv()

    def total_rays(zs, zr, index):
        v = zs[nz - 1, index]
        for t in range(nz - 1):
            v = v + zr[t, index]
        return v * (1.0 / ROI)

    def spread(buf, phase):
        out = [
            send(buf.at[z], buf.at[z], s_z.at[phase, t - 1], r_z.at[phase, t - 1], at_z(t))
            for t in range(1, nz)
        ]
        for c in out:
            c.start()
        return out

    def backward(buf, pv, pr, phase):
        pv[...] = jnp.zeros_like(pv)

        @pl.loop(0, nz)
        def _(t):
            off = t + t // 2 - 2 * (t // 3)
            o = lax.rem(z + nz - off, nz)

            @pl.when(t > 0)
            def _():
                send(buf.at[o], buf.at[o], s_z.at[phase, off - 1], r_z.at[phase, off - 1], at_z(1)).wait_recv()

            for g in range(quads):
                hi, lo = split(buf[o, g])
                wide = dot(hi, copy_out[...]) + dot(lo, copy_out[...])
                for i in range(4):
                    dr[g * 4 + i] = wide[:, i * 128 : (i + 1) * 128].reshape(RAYS // 8, 8, 128)

            rows = pl.ds(pl.multiple_of(o * (ns * TR), ns * TR), ns * TR)

            @pl.loop(0, nx)
            def _(u):
                q = lax.rem(x + 1 + u, nx)
                for g in range(quads):
                    for j in range(4):
                        a = g * 4 + j
                        out = None
                        for s in range(slots):
                            first = starts[(q * slots + s) * na + o * ns + a]
                            v = dr[a, pl.ds(first, TR // 8)].reshape(TR, 128)
                            out = v if s == 0 else jnp.where(lane == s, v, out)
                        tile[j * TR : (j + 1) * TR, :] = out
                    hi, lo = split(jnp.transpose(tile[...]))
                    for s in range(slots):
                        th[s, 0:32, g * 128 : (g + 1) * 128] = hi[s * 32 : (s + 1) * 32]
                        th[s, 32:64, g * 128 : (g + 1) * 128] = lo[s * 32 : (s + 1) * 32]
                for s in range(slots):
                    p = q * slots + s
                    both = dot(th[s], w_hi[p, rows, :])
                    low = dot(th[s, 0:32], w_lo[p, rows, :])
                    cols = slice(s * 256, (s + 1) * 256)
                    pv[u, :, cols] = pv[u, :, cols] + (both[:32] + (both[32:] + low))

                @pl.when((t == nz - 1) & (u < nx - 1))
                def _():
                    send(pv.at[u], pr.at[u], s_x.at[phase, u], r_x.at[phase, u], at_x(1 + u)).start()

        for t in range(nx - 1):
            c = send(pv.at[t], pr.at[t], s_x.at[phase, t], r_x.at[phase, t], at_x(1 + t))
            c.wait_send()
            c.wait_recv()
        v = pv[nx - 1]
        for t in range(nx - 1):
            v = v + pr[t]
        return v * (RELAX / (ns * nz * nx))

    for c in loads:
        c.wait()
    modes = filter_forward(img, h_hi, h_lo, table, ping, pong)

    xg[x] = x0[...]
    for c in x_out:
        c.wait()
    load_volume(xg)
    forward(zs0, zr0, 0)

    filter_back(modes, h_hi, h_lo, img, MID0, MID)
    for c in y_mid:
        c.start()
    for base in (0, right0):

        @pl.loop(0, 3)
        def _(i, base=base):
            filter_back(modes, h_hi, h_lo, img, pl.multiple_of(base + i * 256, 128), 256)

        filter_back(modes, h_hi, h_lo, img, base + 768, 128)
    for c in y_side:
        c.start()
    ymid[slab] = img[own_rows, MID0 : MID0 + MID]
    own_out = [
        pltpu.make_async_copy(img.at[own_rows, pl.ds(0, MID0)], res.at[slab, :, pl.ds(0, MID0)], s_loc.at[1]),
        pltpu.make_async_copy(
            img.at[own_rows, pl.ds(right0, rightn)], res.at[slab, :, pl.ds(right0, rightn)], s_loc.at[2]
        ),
    ]
    for c in own_out:
        c.start()
    for c in y_mid:
        c.wait()
    for g in range(quads):
        block = ymid[g * 4 : (g + 1) * 4].reshape(128, MID)
        for h in range(MID // 128):
            yt[g, h * 128 : (h + 1) * 128, :] = jnp.transpose(block[:, h * 128 : (h + 1) * 128])
    end_forward(zs0, zr0, 0)
    inverse = 1.0 / jnp.maximum(total_rays(zs0, zr0, quads), ROW_FLOOR)
    inv_hi, inv_lo = split(inverse)
    for g in range(quads):
        weight[g] = dot(inv_hi, copy_sum[g]) + dot(inv_lo, copy_sum[g])
        dg[z, g] = (yt[g, SKIP : SKIP + RAYS, :] - total_rays(zs0, zr0, g)) * weight[g]
    d_out = spread(dg, 1)
    first = x0[...] + backward(dg, pv0, pr0, 1)
    for c in d_out:
        c.wait_send()
    xh[x] = first
    x_out = [
        send(xh.at[x], xh.at[x], s_x.at[2, t - 1], r_x.at[2, t - 1], at_x(t)) for t in range(1, nx)
    ]
    for c in x_out:
        c.start()
    for c in x_out:
        c.wait()
    load_volume(xh)
    forward(zs1, zr1, 2)
    end_forward(zs1, zr1, 2)
    for g in range(quads):
        diff = yt[g, SKIP : SKIP + RAYS, :] - total_rays(zs1, zr1, g)
        dh[z, g] = diff * weight[g]
        yt[g, SKIP : SKIP + RAYS, :] = diff
    d_out = spread(dh, 3)
    for g in range(quads):
        for h in range(MID // 128):
            turned = jnp.transpose(yt[g, h * 128 : (h + 1) * 128, :])
            rmid[g * 4 : (g + 1) * 4, :, h * 128 : (h + 1) * 128] = turned.reshape(4, 32, 128)
    mid_out = pltpu.make_async_copy(rmid, res.at[:, :, pl.ds(MID0, MID)], s_loc.at[3])
    mid_out.start()
    rec[...] = first + backward(dh, pv1, pr1, 3)
    for c in d_out:
        c.wait_send()

    mid_out.wait()
    for c in own_out + y_side:
        c.wait()


def sirt(starts, offs, cs, image, x0, dims):
    height, width = image.shape
    h_hi, h_lo, table = filter_tables(height, width)
    anywhere = pl.BlockSpec(memory_space=pl.ANY)
    ns, nz, nx = dims
    np_group = 4 * nx
    na = ns * nz
    rows = na * TR
    quads = ns // 4
    dma = pltpu.SemaphoreType.DMA
    vm = pltpu.VMEM
    smem = pl.BlockSpec(memory_space=pltpu.SMEM)
    peers_z = max(nz - 1, 1)
    peers_x = max(nx - 1, 1)
    return pl.pallas_call(
        functools.partial(sirt_kernel, dims),
        out_shape=(
            jax.ShapeDtypeStruct((ns, 32, BAND), F32),
            jax.ShapeDtypeStruct((32, 1024), F32),
        ),
        in_specs=[smem] * 3 + [anywhere] * 4 + [pl.BlockSpec(memory_space=pltpu.VMEM)],
        out_specs=(pl.BlockSpec(memory_space=pl.ANY), pl.BlockSpec(memory_space=pltpu.VMEM)),
        scratch_shapes=[
            vm((height, width), F32),
            vm((height // 128, width + 2 * HALO, 128), F32),
            vm((height // 128, width + 2 * HALO, 128), F32),
            vm(h_hi.shape, BF16),
            vm(h_lo.shape, BF16),
            vm(table.shape, F32),
            vm((RAYS, 512), BF16),
            vm((RAYS, 512), BF16),
            vm((512, 128), BF16),
            vm((quads, 512, 128), BF16),
            vm((128, 512), BF16),
            vm((quads, 128, 128), BF16),
            vm((np_group, rows, 256), BF16),
            vm((np_group, rows, 256), BF16),
            vm((np_group, 128, 256), BF16),
            vm((ns, (np_group * STRIDE + LEAD) // 8, 8, 128), F32),
            vm((nx, 32, 1024), F32),
            vm((nx, 32, 1024), F32),
            vm((nz, quads + 1, RAYS, 128), F32),
            vm((peers_z, quads + 1, RAYS, 128), F32),
            vm((nz, quads, RAYS, 128), F32),
            vm((peers_z, quads, RAYS, 128), F32),
            vm((nz, quads, RAYS, 128), F32),
            vm((nz, quads, RAYS, 128), F32),
            vm((ns, RAYS // 8, 8, 128), F32),
            vm((128, 128), F32),
            vm((4, 64, ns * TR), BF16),
            vm((nx, 32, 1024), F32),
            vm((peers_x, 32, 1024), F32),
            vm((nx, 32, 1024), F32),
            vm((peers_x, 32, 1024), F32),
            vm((ns, 32, MID), F32),
            vm((quads, MID, 128), F32),
            vm((quads, RAYS, 128), F32),
            vm((ns, 32, MID), F32),
            dma((ns - 1,)),
            dma((ns - 1,)),
            dma((ns - 1,)),
            dma((ns - 1,)),
            dma((ns - 1,)),
            dma((ns - 1,)),
            dma((4, peers_x)),
            dma((4, peers_x)),
            dma((4, peers_z)),
            dma((4, peers_z)),
            dma((8,)),
        ],
        compiler_params=pltpu.CompilerParams(
            collective_id=0, has_side_effects=True, vmem_limit_bytes=62 << 20
        ),
        name="sirt",
    )(starts, offs, cs, image, jnp.asarray(h_hi), jnp.asarray(h_lo), jnp.asarray(table), x0)


def tile_tables(angles, vol_list, z, x, nz, nx):
    theta = lax.dynamic_index_in_dim(angles.reshape(-1, nz, nx), x, 2, keepdims=False)
    theta = jnp.transpose(theta).reshape(-1)
    ids = lax.dynamic_slice_in_dim(vol_list, z * 4 * nx, 4 * nx)
    cosine = jnp.cos(theta)
    sine = jnp.sin(theta)
    centre_x = (ids // PGRID).astype(F32) * 16.0 + 7.5 - HALF_ROI
    centre_y = (ids % PGRID).astype(F32) * 16.0 + 7.5 - HALF_ROI
    centre = HALF_BAND + centre_x[:, None] * cosine[None, :] + centre_y[:, None] * sine[None, :]
    first = jnp.floor(centre - 11.61).astype(jnp.int32) + 1
    start = first // 8
    offs = (start * 8).astype(F32) - centre
    return (start - RAY0 // 8).reshape(-1), offs.reshape(-1), jnp.concatenate([cosine, sine])


def local(dims, intensity, angles, volume, vol_list):
    ns, nz, nx = dims
    rank = lax.axis_index("ray")
    height = intensity.shape[2]
    starts, offs, cs = tile_tables(angles, vol_list, rank // nx, rank % nx, nz, nx)
    res, rec = sirt(starts, offs, cs, intensity.reshape(height, BAND), volume.reshape(32, 1024), dims)
    return rec.reshape(volume.shape), res[:, None]


def make(mesh, dims):
    placed = (P("slab", "ray", None, None), P(), P("slab", "ray", None), P())
    return jax.shard_map(
        functools.partial(local, dims),
        mesh=mesh,
        in_specs=placed,
        out_specs=(P("slab", "ray", None), P(None, "ray", "slab", None)),
        check_vma=False,
    )


def solution(mesh):
    return make(mesh, (mesh.shape["slab"], 4, mesh.shape["ray"] // 4))
```

```python
import functools

import jax
import jax.numpy as jnp
import numpy as np
from jax import lax
from jax.experimental import pallas as pl
from jax.experimental.pallas import tpu as pltpu
from jax.sharding import PartitionSpec as P

BAND = 2048
PGRID = 8
ROI = 128
HALF_ROI = (ROI - 1) / 2.0
HALF_BAND = (BAND - 1) / 2.0
STRENGTH = 10.0
RELAX = 1.8
ROW_FLOOR = 0.25
MESH = pl.DeviceIdType.MESH

TR = 32
MID0 = 896
MID = 256
RAY0 = 928
RAYS = 192
SKIP = RAY0 - MID0
STRIDE = RAYS
LEAD = RAYS - TR
F32 = jnp.float32
BF16 = jnp.bfloat16
HALO = 64


def dot(a, b):
    return lax.dot_general(a, b, (((1,), (0,)), ((), ())), preferred_element_type=F32)


def dot_nt(a, b):
    return lax.dot_general(a, b, (((1,), (1,)), ((), ())), preferred_element_type=F32)


def dot_tn(a, b):
    return lax.dot_general(a, b, (((0,), (0,)), ((), ())), preferred_element_type=F32)


def split(v):
    hi = v.astype(BF16)
    return hi, (v - hi.astype(F32)).astype(BF16)


def filter_tables(height, width):
    m = np.arange(height)
    ang = 2.0 * np.pi * (np.outer(m, m) % height) / height
    had = (np.cos(ang) + np.sin(ang)) / np.sqrt(height)
    beta = 1.0 + STRENGTH * (2.0 - 2.0 * np.cos(2.0 * np.pi * m / height)) + 2.0 * STRENGTH
    half = beta / (2.0 * STRENGTH)
    root = half - np.sqrt(half * half - 1.0)
    scale = root / STRENGTH / (1.0 - root**width) ** 2
    steps = int(np.log2(width))
    table = np.zeros((16, height))
    power = root
    for k in range(steps):
        table[k] = power / (1.0 + power * power)
        scale = scale * (1.0 + power * power)
        power = power * power
    table[15] = scale
    return np.concatenate([had, table]).astype(np.float32)


def filter_forward(img, h_hi, h_lo, table, ping, pong):
    height, width = img.shape
    chunk = 256
    halves = height // 128

    @pl.loop(0, width // chunk)
    def _(c):
        cols = pl.ds(pl.multiple_of(c * chunk, chunk), chunk)
        rows = pl.ds(pl.multiple_of(HALO + c * chunk, 8), chunk)
        v_hi, v_lo = split(jnp.transpose(1.0 - img[:, cols]))
        v = dot(v_hi, h_hi[...]) + (dot(v_lo, h_hi[...]) + dot(v_hi, h_lo[...]))
        for h in range(halves):
            ping[h, rows, :] = v[:, h * 128 : (h + 1) * 128]

    def row(k, h):
        return jnp.broadcast_to(table[k : k + 1, h * 128 : (h + 1) * 128], (8, 128))

    source, target = ping, pong
    step, k = 1, 0
    while step <= HALO:
        for h in range(halves):
            source[h, 0:HALO, :] = source[h, width : width + HALO, :]
            source[h, width + HALO : width + 2 * HALO, :] = source[h, HALO : 2 * HALO, :]
            rate = row(k, h)

            @pl.loop(0, width // 128)
            def _(b, h=h, step=step, source=source, target=target, rate=rate):
                for i in range(16):
                    at = b * 128 + HALO + 8 * i
                    here = source[h, pl.ds(at, 8), :]
                    near = source[h, pl.ds(at - step, 8), :] + source[h, pl.ds(at + step, 8), :]
                    target[h, pl.ds(at, 8), :] = here + rate * near

        source, target = target, source
        step *= 2
        k += 1

    for h in range(halves):
        rates = [row(j, h) for j in range(k, k + 4)]
        scale = row(15, h)

        @pl.loop(0, 16)
        def _(i, h=h, rates=rates, scale=scale):
            v = [source[h, pl.ds(HALO + b * 128 + 8 * i, 8), :] for b in range(16)]
            for j, rate in zip((1, 2, 4, 8), rates):
                v = [v[b] + rate * (v[b - j] + v[(b + j) % 16]) for b in range(16)]
            for b in range(16):
                target[h, pl.ds(HALO + b * 128 + 8 * i, 8), :] = v[b] * scale

    return target


def filter_back(modes, h_hi, h_lo, out, first, count):
    rows = pl.ds(HALO + first, count)
    v = jnp.concatenate([modes[h, rows, :] for h in range(out.shape[0] // 128)], axis=1)
    v_hi, v_lo = split(v)
    v = dot_nt(h_hi[...], v_hi) + (dot_nt(h_hi[...], v_lo) + dot_nt(h_lo[...], v_hi))
    out[:, pl.ds(first, count)] = -jnp.log(1.0 - v)


def sirt_kernel(
    dims,
    starts,
    offs,
    cs,
    image,
    table_in,
    volume,
    res,
    rec,
    x0,
    img,
    ping,
    pong,
    h_hi,
    h_lo,
    parts_hi,
    parts_lo,
    pick,
    copy_out,
    copy_sum,
    sums,
    w_hi,
    w_lo,
    xb,
    pad,
    xg,
    xh,
    zs0,
    zr0,
    zs1,
    zr1,
    dg,
    dh,
    dr,
    tile,
    th,
    pv0,
    pr0,
    pv1,
    pr1,
    ymid,
    yt,
    weight,
    zsum,
    zrsum,
    s_sum,
    r_sum,
    s_mid,
    r_mid,
    s_left,
    r_left,
    s_right,
    r_right,
    s_x,
    r_x,
    s_z,
    r_z,
    s_loc,
):
    ns, nz, nx = dims
    slots = 4
    np_group = slots * nx
    na = ns * nz
    quads = ns // 4
    right0 = MID0 + MID
    rightn = BAND - right0
    slab = lax.axis_index("slab")
    ray = lax.axis_index("ray")
    z = ray // nx
    x = lax.rem(ray, nx)

    def at_slab(t):
        return {"slab": lax.rem(slab + t, ns), "ray": ray}

    def at_z(t):
        return {"slab": slab, "ray": lax.rem(z + t, nz) * nx + x}

    def at_x(t):
        return {"slab": slab, "ray": z * nx + lax.rem(x + t, nx)}

    loads = [
        pltpu.make_async_copy(image, img, s_loc.at[7]),
    ]
    x_loads = [
        pltpu.make_async_copy(volume.at[:, s, :], x0.at[:, pl.ds(s * 256, 256)], s_loc.at[s])
        for s in range(slots)
    ]
    for c in x_loads + loads:
        c.start()
    barrier = pltpu.get_barrier_semaphore()
    for t in range(1, nx):
        pl.semaphore_signal(barrier, inc=1, device_id=at_x(t), device_id_type=MESH)
    for t in range(1, nz):
        pl.semaphore_signal(barrier, inc=1, device_id=at_z(t), device_id_type=MESH)
    for t in range(1, ns):
        pl.semaphore_signal(barrier, inc=1, device_id=at_slab(t), device_id_type=MESH)
    pl.semaphore_wait(barrier, nx + nz + ns - 3)

    def send(src, dst, ssem, rsem, device):
        return pltpu.make_async_remote_copy(
            src_ref=src, dst_ref=dst, send_sem=ssem, recv_sem=rsem, device_id=device, device_id_type=MESH
        )

    for c in x_loads:
        c.wait()
    x_out = [
        send(x0, xg.at[x], s_x.at[0, t - 1], r_x.at[0, t - 1], at_x(t)) for t in range(1, nx)
    ]
    for c in x_out:
        c.start()
    y_mid, y_side = [], []
    own_rows = pl.ds(pl.multiple_of(slab * 32, 32), 32)
    for t in range(1, ns):
        to = pl.ds(pl.multiple_of(lax.rem(slab + t, ns) * 32, 32), 32)
        y_mid.append(
            send(
                img.at[to, pl.ds(MID0, MID)], ymid.at[slab], s_mid.at[t - 1], r_mid.at[t - 1], at_slab(t)
            )
        )
        y_side.append(
            send(
                img.at[to, pl.ds(0, MID0)],
                res.at[slab, :, pl.ds(0, MID0)],
                s_left.at[t - 1],
                r_left.at[t - 1],
                at_slab(t),
            )
        )
        y_side.append(
            send(
                img.at[to, pl.ds(right0, rightn)],
                res.at[slab, :, pl.ds(right0, rightn)],
                s_right.at[t - 1],
                r_right.at[t - 1],
                at_slab(t),
            )
        )

    height = img.shape[0]
    h_hi[...], h_lo[...] = split(table_in[0:height, :])
    table = table_in.at[pl.ds(height, 16), :]

    vox = lax.broadcasted_iota(jnp.int32, (1, 256), 1)
    dx = (vox // 16).astype(F32) - 7.5
    dy = lax.rem(vox, 16).astype(F32) - 7.5
    lane_ray = lax.broadcasted_iota(jnp.int32, (TR, 256), 0).astype(F32)

    @pl.loop(0, na)
    def _(a):
        base = lane_ray - (dx * cs[0, a] + dy * cs[8, a])
        rows = pl.ds(pl.multiple_of(a * TR, TR), TR)

        @pl.loop(0, np_group)
        def _(p):
            hat = jnp.maximum(0.0, 1.0 - jnp.abs(base + offs[p, a]))
            hi, lo = split(hat)
            w_hi[p, rows, :] = hi
            w_lo[p, rows, :] = lo

    @pl.loop(0, ns)
    def _(a):
        for p in range(np_group):
            pad[a, pl.ds(p * STRIDE // 8, LEAD // 8)] = jnp.zeros((LEAD // 8, 8, 128), F32)
        pad[a, pl.ds(np_group * STRIDE // 8, LEAD // 8)] = jnp.zeros((LEAD // 8, 8, 128), F32)

    @pl.loop(0, np_group)
    def _(p):
        xb[p, 64:96, :] = jnp.ones((32, 256), BF16)
        xb[p, 96:128, :] = jnp.zeros((32, 256), BF16)

    lane = lax.broadcasted_iota(jnp.int32, (1, 128), 1) // 32

    def one_hot(shape, test):
        r = lax.broadcasted_iota(jnp.int32, shape, 0)
        c = lax.broadcasted_iota(jnp.int32, shape, 1)
        return jnp.where(test(r, c), 1.0, 0.0).astype(BF16)

    for g in range(quads):
        pick[g, :, 0:128] = one_hot(
            (512, 128), lambda r, c: (r % 128 < 64) & (r % 32 == c % 32) & (r // 128 == c // 32)
        )
        pick[g, :, 128:256] = one_hot(
            (512, 128), lambda r, c, g=g: (r % 128 == 64) & (g * 4 + r // 128 == c)
        )
        copy_sum[g] = one_hot((16, 128), lambda r, c, g=g: r == g * 4 + c // 32)
    copy_out[...] = one_hot((128, 512), lambda r, c: (r // 32 == c // 128) & (r % 32 == c % 32))

    def load_volume(source):
        for q in range(nx):
            for s in range(slots):
                hi, lo = split(source[q, :, pl.ds(s * 256, 256)])
                xb[q * slots + s, 0:32, :] = hi
                xb[q * slots + s, 32:64, :] = lo

    def forward(zs, zr, phase):
        with_sums = phase == 0

        @pl.loop(0, nz)
        def _(t):
            o = lax.rem(z + 1 + t, nz)
            rows = pl.ds(pl.multiple_of(o * (ns * TR), ns * TR), ns * TR)

            @pl.loop(0, np_group, unroll=8)
            def _(p):
                part = dot_nt(w_hi[p, rows, :], xb[p]) + dot_nt(w_lo[p, rows, :], xb[p])
                at = pl.ds(p * (STRIDE // 8) + LEAD // 8, TR // 8)
                for a in range(ns):
                    pad[a, at] = part[a * TR : (a + 1) * TR].reshape(TR // 8, 8, 128)

            @pl.loop(0, quads)
            def _(g):
                for i in range(4):
                    a = g * 4 + i
                    acc = jnp.zeros((RAYS, 128), F32)
                    for p in range(np_group):
                        first = (p * STRIDE + LEAD) // 8 - starts[p, o * ns + a]
                        acc = acc + pad[a, pl.ds(first, RAYS // 8)].reshape(RAYS, 128)
                    hi, lo = split(acc)
                    parts_hi[:, i * 128 : (i + 1) * 128] = hi
                    parts_lo[:, i * 128 : (i + 1) * 128] = lo
                if with_sums:
                    part = dot(parts_hi[...], pick[g]) + dot(parts_lo[...], pick[g])
                    zs[t, g] = part[:, :128]
                    sums[...] = jnp.where(g == 0, part[:, 128:], part[:, 128:] + sums[...])
                else:
                    zs[t, g] = dot(parts_hi[...], pick[0, :, 0:128]) + dot(parts_lo[...], pick[0, :, 0:128])

            if with_sums:
                zsum[t, :, 0:128] = jnp.transpose(sums[0:128])[0:ns]
                zsum[t, :, 128:RAYS] = jnp.transpose(sums[128:RAYS])[0:ns]
                zsum[t, :, RAYS:256] = jnp.ones((ns, 256 - RAYS), F32)

            @pl.when(t < nz - 1)
            def _():
                send(zs.at[t], zr.at[t], s_z.at[phase, t], r_z.at[phase, t], at_z(1 + t)).start()
                if with_sums:
                    send(zsum.at[t], zrsum.at[t], s_sum.at[t], r_sum.at[t], at_z(1 + t)).start()

    def end_forward(zs, zr, phase):
        for t in range(nz - 1):
            c = send(zs.at[t], zr.at[t], s_z.at[phase, t], r_z.at[phase, t], at_z(1 + t))
            c.wait_send()
            c.wait_recv()
            if phase == 0:
                c = send(zsum.at[t], zrsum.at[t], s_sum.at[t], r_sum.at[t], at_z(1 + t))
                c.wait_send()
                c.wait_recv()

    def total_rays(zs, zr, index):
        v = zs[nz - 1, index]
        for t in range(nz - 1):
            v = v + zr[t, index]
        return v * (1.0 / ROI)

    def spread(buf, phase):
        out = [
            send(buf.at[z], buf.at[z], s_z.at[phase, t - 1], r_z.at[phase, t - 1], at_z(t))
            for t in range(1, nz)
        ]
        for c in out:
            c.start()
        return out

    def backward(buf, pv, pr, phase):
        pv[...] = jnp.zeros_like(pv)

        @pl.loop(0, nz)
        def _(t):
            off = t + t // 2 - 2 * (t // 3)
            o = lax.rem(z + nz - off, nz)

            @pl.when(t > 0)
            def _():
                send(buf.at[o], buf.at[o], s_z.at[phase, off - 1], r_z.at[phase, off - 1], at_z(1)).wait_recv()

            for g in range(quads):
                hi, lo = split(buf[o, g])
                wide = dot(hi, copy_out[...]) + dot(lo, copy_out[...])
                for i in range(4):
                    dr[g * 4 + i] = wide[:, i * 128 : (i + 1) * 128].reshape(RAYS // 8, 8, 128)

            rows = pl.ds(pl.multiple_of(o * (ns * TR), ns * TR), ns * TR)

            @pl.loop(0, nx)
            def _(u):
                q = lax.rem(x + 1 + u, nx)
                for g in range(quads):
                    for j in range(4):
                        a = g * 4 + j
                        out = None
                        for s in range(slots):
                            first = starts[q * slots + s, o * ns + a]
                            v = dr[a, pl.ds(first, TR // 8)].reshape(TR, 128)
                            out = v if s == 0 else jnp.where(lane == s, v, out)
                        tile[j * TR : (j + 1) * TR, :] = out
                    hi, lo = split(jnp.transpose(tile[...]))
                    for s in range(slots):
                        th[s, 0:32, g * 128 : (g + 1) * 128] = hi[s * 32 : (s + 1) * 32]
                        th[s, 32:64, g * 128 : (g + 1) * 128] = lo[s * 32 : (s + 1) * 32]
                for s in range(slots):
                    p = q * slots + s
                    both = dot(th[s], w_hi[p, rows, :])
                    low = dot(th[s, 0:32], w_lo[p, rows, :])
                    cols = slice(s * 256, (s + 1) * 256)
                    pv[u, :, cols] = pv[u, :, cols] + (both[:32] + (both[32:] + low))

                @pl.when((t == nz - 1) & (u < nx - 1))
                def _():
                    send(pv.at[u], pr.at[u], s_x.at[phase, u], r_x.at[phase, u], at_x(1 + u)).start()

        for t in range(nx - 1):
            c = send(pv.at[t], pr.at[t], s_x.at[phase, t], r_x.at[phase, t], at_x(1 + t))
            c.wait_send()
            c.wait_recv()
        v = pv[nx - 1]
        for t in range(nx - 1):
            v = v + pr[t]
        return v * (RELAX / (ns * nz * nx))

    for c in loads:
        c.wait()
    modes = filter_forward(img, h_hi, h_lo, table, ping, pong)

    xg[x] = x0[...]
    for c in x_out:
        c.wait()
    load_volume(xg)
    forward(zs0, zr0, 0)

    filter_back(modes, h_hi, h_lo, img, MID0, MID)
    for c in y_mid:
        c.start()
    for base in (0, right0):

        @pl.loop(0, 3)
        def _(i, base=base):
            filter_back(modes, h_hi, h_lo, img, pl.multiple_of(base + i * 256, 128), 256)

        filter_back(modes, h_hi, h_lo, img, base + 768, 128)
    for c in y_side:
        c.start()
    ymid[slab] = img[own_rows, MID0 : MID0 + MID]
    res[slab] = img[own_rows, :]
    for c in y_mid:
        c.wait()
    for g in range(quads):
        block = ymid[g * 4 : (g + 1) * 4].reshape(128, MID)
        for h in range(MID // 128):
            yt[g, h * 128 : (h + 1) * 128, :] = jnp.transpose(block[:, h * 128 : (h + 1) * 128])
    end_forward(zs0, zr0, 0)
    total = zsum[nz - 1]
    for t in range(nz - 1):
        total = total + zrsum[t]
    inverse = 1.0 / jnp.maximum(total * (1.0 / ROI), ROW_FLOOR)
    inv_hi, inv_lo = split(jnp.concatenate([inverse, jnp.zeros_like(inverse)], axis=0))
    for g in range(quads):
        weight[g] = (dot_tn(inv_hi, copy_sum[g]) + dot_tn(inv_lo, copy_sum[g]))[:RAYS]
    for g in range(quads):
        dg[z, g] = (yt[g, SKIP : SKIP + RAYS, :] - total_rays(zs0, zr0, g)) * weight[g]
    d_out = spread(dg, 1)
    first = x0[...] + backward(dg, pv0, pr0, 1)
    for c in d_out:
        c.wait_send()
    xh[x] = first
    x_out = [
        send(xh.at[x], xh.at[x], s_x.at[2, t - 1], r_x.at[2, t - 1], at_x(t)) for t in range(1, nx)
    ]
    for c in x_out:
        c.start()
    for c in x_out:
        c.wait()
    load_volume(xh)
    forward(zs1, zr1, 2)
    end_forward(zs1, zr1, 2)
    for g in range(quads):
        diff = yt[g, SKIP : SKIP + RAYS, :] - total_rays(zs1, zr1, g)
        dh[z, g] = diff * weight[g]
        yt[g, SKIP : SKIP + RAYS, :] = diff
    d_out = spread(dh, 3)
    for g in range(quads):
        for h in range(MID // 128):
            turned = jnp.transpose(yt[g, h * 128 : (h + 1) * 128, :]).reshape(4, 32, 128)
            res[g * 4 : (g + 1) * 4, :, MID0 + h * 128 : MID0 + (h + 1) * 128] = turned
    last = first + backward(dh, pv1, pr1, 3)
    for s in range(slots):
        rec[:, s, :] = last[:, s * 256 : (s + 1) * 256]
    for c in d_out:
        c.wait_send()

    for c in y_side:
        c.wait()


def sirt(starts, offs, cs, image, volume, dims):
    height, width = image.shape
    table = filter_tables(height, width)
    anywhere = pl.BlockSpec(memory_space=pl.ANY)
    ns, nz, nx = dims
    np_group = 4 * nx
    na = ns * nz
    rows = na * TR
    quads = ns // 4
    dma = pltpu.SemaphoreType.DMA
    vm = pltpu.VMEM
    smem = pl.BlockSpec(memory_space=pltpu.SMEM)
    peers_z = max(nz - 1, 1)
    peers_x = max(nx - 1, 1)
    return pl.pallas_call(
        functools.partial(sirt_kernel, dims),
        out_shape=(
            jax.ShapeDtypeStruct((ns, 32, BAND), F32),
            jax.ShapeDtypeStruct(volume.shape, F32),
        ),
        in_specs=[smem] * 3 + [anywhere, pl.BlockSpec(memory_space=pltpu.VMEM), anywhere],
        out_specs=(pl.BlockSpec(memory_space=pltpu.VMEM), pl.BlockSpec(memory_space=pltpu.VMEM)),
        scratch_shapes=[
            vm((32, 1024), F32),
            vm((height, width), F32),
            vm((height // 128, width + 2 * HALO, 128), F32),
            vm((height // 128, width + 2 * HALO, 128), F32),
            vm((height, height), BF16),
            vm((height, height), BF16),
            vm((RAYS, 512), BF16),
            vm((RAYS, 512), BF16),
            vm((quads, 512, 256), BF16),
            vm((128, 512), BF16),
            vm((quads, 16, 128), BF16),
            vm((RAYS, 128), F32),
            vm((np_group, rows, 256), BF16),
            vm((np_group, rows, 256), BF16),
            vm((np_group, 128, 256), BF16),
            vm((ns, (np_group * STRIDE + LEAD) // 8, 8, 128), F32),
            vm((nx, 32, 1024), F32),
            vm((nx, 32, 1024), F32),
            vm((nz, quads, RAYS, 128), F32),
            vm((peers_z, quads, RAYS, 128), F32),
            vm((nz, quads, RAYS, 128), F32),
            vm((peers_z, quads, RAYS, 128), F32),
            vm((nz, quads, RAYS, 128), F32),
            vm((nz, quads, RAYS, 128), F32),
            vm((ns, RAYS // 8, 8, 128), F32),
            vm((128, 128), F32),
            vm((4, 64, ns * TR), BF16),
            vm((nx, 32, 1024), F32),
            vm((peers_x, 32, 1024), F32),
            vm((nx, 32, 1024), F32),
            vm((peers_x, 32, 1024), F32),
            vm((ns, 32, MID), F32),
            vm((quads, MID, 128), F32),
            vm((quads, RAYS, 128), F32),
            vm((nz, ns, 256), F32),
            vm((peers_z, ns, 256), F32),
            dma((peers_z,)),
            dma((peers_z,)),
            dma((ns - 1,)),
            dma((ns - 1,)),
            dma((ns - 1,)),
            dma((ns - 1,)),
            dma((ns - 1,)),
            dma((ns - 1,)),
            dma((4, peers_x)),
            dma((4, peers_x)),
            dma((4, peers_z)),
            dma((4, peers_z)),
            dma((8,)),
        ],
        compiler_params=pltpu.CompilerParams(
            collective_id=0, has_side_effects=True, vmem_limit_bytes=50 << 20
        ),
        name="sirt",
    )(starts, offs, cs, image, jnp.asarray(table), volume)


def tables_kernel(dims, angles, ids, starts, offs, cs):
    ns, nz, nx = dims
    ray = lax.axis_index("ray")
    z = ray // nx
    x = lax.rem(ray, nx)
    shape = (4 * nx, 128)
    row = lax.broadcasted_iota(jnp.int32, shape, 0)
    lane = lax.broadcasted_iota(jnp.int32, shape, 1)
    theta = jnp.zeros(shape, F32)
    for a in range(ns * nz):
        theta = jnp.where(lane == a, angles[a % ns, a // ns * nx + x], theta)
    patch = jnp.zeros(shape, jnp.int32)
    for p in range(4 * nx):
        patch = jnp.where(row == p, ids[z * 4 * nx + p], patch)
    cosine = jnp.cos(theta)
    sine = jnp.sin(theta)
    centre_x = (patch // PGRID).astype(F32) * 16.0 + 7.5 - HALF_ROI
    centre_y = (patch % PGRID).astype(F32) * 16.0 + 7.5 - HALF_ROI
    centre = HALF_BAND + centre_x * cosine + centre_y * sine
    first = jnp.floor(centre - 11.61).astype(jnp.int32) + 1
    start = first // 8
    starts[...] = start - RAY0 // 8
    offs[...] = (start * 8).astype(F32) - centre
    cs[0:8, :] = cosine[0:8]
    cs[8:16, :] = sine[0:8]


def tile_tables(angles, vol_list, dims):
    shape = (4 * dims[2], 128)
    return pl.pallas_call(
        functools.partial(tables_kernel, dims),
        out_shape=(
            jax.ShapeDtypeStruct(shape, jnp.int32),
            jax.ShapeDtypeStruct(shape, F32),
            jax.ShapeDtypeStruct((16, 128), F32),
        ),
        in_specs=[pl.BlockSpec(memory_space=pltpu.SMEM)] * 2,
        out_specs=(pl.BlockSpec(memory_space=pltpu.VMEM),) * 3,
        compiler_params=pltpu.CompilerParams(vmem_limit_bytes=4 << 20),
        name="tile_tables",
    )(angles, vol_list)


def local(dims, intensity, angles, volume, vol_list):
    ns, nz, nx = dims
    height = intensity.shape[2]
    starts, offs, cs = tile_tables(angles, vol_list, dims)
    res, rec = sirt(starts, offs, cs, intensity.reshape(height, BAND), volume, dims)
    return rec, res[:, None]


def make(mesh, dims):
    placed = (P("slab", "ray", None, None), P(), P("slab", "ray", None), P())
    return jax.shard_map(
        functools.partial(local, dims),
        mesh=mesh,
        in_specs=placed,
        out_specs=(P("slab", "ray", None), P(None, "ray", "slab", None)),
        check_vma=False,
    )


def solution(mesh):
    return make(mesh, (mesh.shape["slab"], 4, mesh.shape["ray"] // 4))
```

```python
import functools

import jax
import jax.numpy as jnp
import numpy as np
from jax import lax
from jax.experimental import pallas as pl
from jax.experimental.pallas import tpu as pltpu
from jax.sharding import PartitionSpec as P

BAND = 2048
PGRID = 8
ROI = 128
HALF_ROI = (ROI - 1) / 2.0
HALF_BAND = (BAND - 1) / 2.0
STRENGTH = 10.0
RELAX = 1.8
ROW_FLOOR = 0.25
MESH = pl.DeviceIdType.MESH

TR = 32
MID0 = 896
MID = 256
RAY0 = 928
RAYS = 192
SKIP = RAY0 - MID0
STRIDE = RAYS
LEAD = RAYS - TR
F32 = jnp.float32
BF16 = jnp.bfloat16
HALO = 64


def dot(a, b):
    return lax.dot_general(a, b, (((1,), (0,)), ((), ())), preferred_element_type=F32)


def dot_nt(a, b):
    return lax.dot_general(a, b, (((1,), (1,)), ((), ())), preferred_element_type=F32)


def dot_tn(a, b):
    return lax.dot_general(a, b, (((0,), (0,)), ((), ())), preferred_element_type=F32)


def split(v):
    hi = v.astype(BF16)
    return hi, (v - hi.astype(F32)).astype(BF16)


def filter_tables(height, width):
    m = np.arange(height)
    ang = 2.0 * np.pi * (np.outer(m, m) % height) / height
    had = (np.cos(ang) + np.sin(ang)) / np.sqrt(height)
    beta = 1.0 + STRENGTH * (2.0 - 2.0 * np.cos(2.0 * np.pi * m / height)) + 2.0 * STRENGTH
    half = beta / (2.0 * STRENGTH)
    root = half - np.sqrt(half * half - 1.0)
    scale = root / STRENGTH / (1.0 - root**width) ** 2
    steps = int(np.log2(width))
    table = np.zeros((16, height))
    power = root
    for k in range(steps):
        table[k] = power / (1.0 + power * power)
        scale = scale * (1.0 + power * power)
        power = power * power
    table[15] = scale
    return np.concatenate([had, table]).astype(np.float32)


def filter_forward(img, h_hi, h_lo, table, ping, pong):
    height, width = img.shape
    chunk = 256
    halves = height // 128

    @pl.loop(0, width // chunk)
    def _(c):
        cols = pl.ds(pl.multiple_of(c * chunk, chunk), chunk)
        rows = pl.ds(pl.multiple_of(HALO + c * chunk, 8), chunk)
        v_hi, v_lo = split(jnp.transpose(1.0 - img[:, cols]))
        v = dot(v_hi, h_hi[...]) + (dot(v_lo, h_hi[...]) + dot(v_hi, h_lo[...]))
        for h in range(halves):
            ping[h, rows, :] = v[:, h * 128 : (h + 1) * 128]

    def row(k, h):
        return jnp.broadcast_to(table[k : k + 1, h * 128 : (h + 1) * 128], (8, 128))

    source, target = ping, pong
    step, k = 1, 0
    while step <= HALO:
        for h in range(halves):
            source[h, 0:HALO, :] = source[h, width : width + HALO, :]
            source[h, width + HALO : width + 2 * HALO, :] = source[h, HALO : 2 * HALO, :]
            rate = row(k, h)

            @pl.loop(0, width // 128)
            def _(b, h=h, step=step, source=source, target=target, rate=rate):
                for i in range(16):
                    at = b * 128 + HALO + 8 * i
                    here = source[h, pl.ds(at, 8), :]
                    near = source[h, pl.ds(at - step, 8), :] + source[h, pl.ds(at + step, 8), :]
                    target[h, pl.ds(at, 8), :] = here + rate * near

        source, target = target, source
        step *= 2
        k += 1

    for h in range(halves):
        rates = [row(j, h) for j in range(k, k + 4)]
        scale = row(15, h)

        @pl.loop(0, 16)
        def _(i, h=h, rates=rates, scale=scale):
            v = [source[h, pl.ds(HALO + b * 128 + 8 * i, 8), :] for b in range(16)]
            for j, rate in zip((1, 2, 4, 8), rates):
                v = [v[b] + rate * (v[b - j] + v[(b + j) % 16]) for b in range(16)]
            for b in range(16):
                target[h, pl.ds(HALO + b * 128 + 8 * i, 8), :] = v[b] * scale

    return target


def filter_back(modes, h_hi, h_lo, out, first, count):
    rows = pl.ds(HALO + first, count)
    v = jnp.concatenate([modes[h, rows, :] for h in range(out.shape[0] // 128)], axis=1)
    v_hi, v_lo = split(v)
    v = dot_nt(h_hi[...], v_hi) + (dot_nt(h_hi[...], v_lo) + dot_nt(h_lo[...], v_hi))
    out[:, pl.ds(first, count)] = -jnp.log(1.0 - v)


def sirt_kernel(
    dims,
    starts,
    offs,
    cs,
    image,
    table_in,
    volume,
    res,
    rec,
    x0,
    img,
    ping,
    pong,
    h_hi,
    h_lo,
    parts_hi,
    parts_lo,
    pick,
    copy_out,
    copy_sum,
    sums,
    w_hi,
    w_lo,
    xb,
    pad,
    xg,
    xh,
    zs0,
    zr0,
    zs1,
    zr1,
    dg,
    dh,
    dr,
    tile,
    th,
    pv0,
    pr0,
    pv1,
    pr1,
    ymid,
    yt,
    weight,
    zsum,
    zrsum,
    s_sum,
    r_sum,
    s_mid,
    r_mid,
    s_left,
    r_left,
    s_right,
    r_right,
    s_x,
    r_x,
    s_z,
    r_z,
    s_loc,
):
    ns, nz, nx = dims
    slots = 4
    np_group = slots * nx
    na = ns * nz
    quads = ns // 4
    right0 = MID0 + MID
    rightn = BAND - right0
    slab = lax.axis_index("slab")
    ray = lax.axis_index("ray")
    z = ray // nx
    x = lax.rem(ray, nx)

    def at_slab(t):
        return {"slab": lax.rem(slab + t, ns), "ray": ray}

    def at_z(t):
        return {"slab": slab, "ray": lax.rem(z + t, nz) * nx + x}

    def at_x(t):
        return {"slab": slab, "ray": z * nx + lax.rem(x + t, nx)}

    loads = [
        pltpu.make_async_copy(image, img, s_loc.at[7]),
    ]
    x_loads = [
        pltpu.make_async_copy(volume.at[:, s, :], x0.at[:, pl.ds(s * 256, 256)], s_loc.at[s])
        for s in range(slots)
    ]
    for c in x_loads + loads:
        c.start()
    barrier = pltpu.get_barrier_semaphore()
    for t in range(1, nx):
        pl.semaphore_signal(barrier, inc=1, device_id=at_x(t), device_id_type=MESH)
    for t in range(1, nz):
        pl.semaphore_signal(barrier, inc=1, device_id=at_z(t), device_id_type=MESH)
    for t in range(1, ns):
        pl.semaphore_signal(barrier, inc=1, device_id=at_slab(t), device_id_type=MESH)
    pl.semaphore_wait(barrier, nx + nz + ns - 3)

    def send(src, dst, ssem, rsem, device):
        return pltpu.make_async_remote_copy(
            src_ref=src, dst_ref=dst, send_sem=ssem, recv_sem=rsem, device_id=device, device_id_type=MESH
        )

    for c in x_loads:
        c.wait()
    x_out = [
        send(x0, xg.at[x], s_x.at[0, t - 1], r_x.at[0, t - 1], at_x(t)) for t in range(1, nx)
    ]
    for c in x_out:
        c.start()
    y_mid, y_side = [], []
    own_rows = pl.ds(pl.multiple_of(slab * 32, 32), 32)
    for t in range(1, ns):
        to = pl.ds(pl.multiple_of(lax.rem(slab + t, ns) * 32, 32), 32)
        y_mid.append(
            send(
                img.at[to, pl.ds(MID0, MID)], ymid.at[slab], s_mid.at[t - 1], r_mid.at[t - 1], at_slab(t)
            )
        )
        y_side.append(
            send(
                img.at[to, pl.ds(0, MID0)],
                res.at[slab, :, pl.ds(0, MID0)],
                s_left.at[t - 1],
                r_left.at[t - 1],
                at_slab(t),
            )
        )
        y_side.append(
            send(
                img.at[to, pl.ds(right0, rightn)],
                res.at[slab, :, pl.ds(right0, rightn)],
                s_right.at[t - 1],
                r_right.at[t - 1],
                at_slab(t),
            )
        )

    height = img.shape[0]
    h_hi[...], h_lo[...] = split(table_in[0:height, :])
    table = table_in.at[pl.ds(height, 16), :]

    vox = lax.broadcasted_iota(jnp.int32, (1, 256), 1)
    dx = (vox // 16).astype(F32) - 7.5
    dy = lax.rem(vox, 16).astype(F32) - 7.5
    lane_ray = lax.broadcasted_iota(jnp.int32, (TR, 256), 0).astype(F32)

    @pl.loop(0, na)
    def _(a):
        base = lane_ray - (dx * cs[0, a] + dy * cs[8, a])
        rows = pl.ds(pl.multiple_of(a * TR, TR), TR)

        @pl.loop(0, np_group)
        def _(p):
            hat = jnp.maximum(0.0, 1.0 - jnp.abs(base + offs[p, a]))
            hi, lo = split(hat)
            w_hi[p, rows, :] = hi
            w_lo[p, rows, :] = lo

    @pl.loop(0, ns)
    def _(a):
        for p in range(np_group):
            pad[a, pl.ds(p * STRIDE // 8, LEAD // 8)] = jnp.zeros((LEAD // 8, 8, 128), F32)
        pad[a, pl.ds(np_group * STRIDE // 8, LEAD // 8)] = jnp.zeros((LEAD // 8, 8, 128), F32)

    @pl.loop(0, np_group)
    def _(p):
        xb[p, 64:96, :] = jnp.ones((32, 256), BF16)
        xb[p, 96:128, :] = jnp.zeros((32, 256), BF16)

    lane = lax.broadcasted_iota(jnp.int32, (1, 128), 1) // 32

    def one_hot(shape, test):
        r = lax.broadcasted_iota(jnp.int32, shape, 0)
        c = lax.broadcasted_iota(jnp.int32, shape, 1)
        return jnp.where(test(r, c), 1.0, 0.0).astype(BF16)

    for g in range(quads):
        pick[g, :, 0:128] = one_hot(
            (512, 128), lambda r, c: (r % 128 < 64) & (r % 32 == c % 32) & (r // 128 == c // 32)
        )
        pick[g, :, 128:256] = one_hot(
            (512, 128), lambda r, c, g=g: (r % 128 == 64) & (g * 4 + r // 128 == c)
        )
        copy_sum[g] = one_hot((16, 128), lambda r, c, g=g: r == g * 4 + c // 32)
    copy_out[...] = one_hot((128, 512), lambda r, c: (r // 32 == c // 128) & (r % 32 == c % 32))

    def load_shard(source, q):
        for s in range(slots):
            hi, lo = split(source[q, :, pl.ds(s * 256, 256)])
            xb[q * slots + s, 0:32, :] = hi
            xb[q * slots + s, 32:64, :] = lo

    def ahead(t):
        return 2 - t + 3 * (t // 2) + 2 * (t // 3)

    def behind(t):
        return t + t // 2 - 2 * (t // 3)

    def forward(zs, zr, phase):
        with_sums = phase == 0

        @pl.loop(0, nz)
        def _(t):
            o = lax.rem(z + ahead(t), nz)
            rows = pl.ds(pl.multiple_of(o * (ns * TR), ns * TR), ns * TR)

            def weigh(p):
                part = dot_nt(w_hi[p, rows, :], xb[p]) + dot_nt(w_lo[p, rows, :], xb[p])
                at = pl.ds(p * (STRIDE // 8) + LEAD // 8, TR // 8)
                for a in range(ns):
                    pad[a, at] = part[a * TR : (a + 1) * TR].reshape(TR // 8, 8, 128)

            def weigh_all():
                @pl.loop(0, np_group, unroll=8)
                def _(p):
                    weigh(p)

            if phase == 0:
                weigh_all()
            else:
                pl.when(t > 0)(weigh_all)

                @pl.when(t == 0)
                def _():
                    @pl.loop(0, nx)
                    def _(u):
                        off = behind(u)
                        q = lax.rem(x + nx - off, nx)

                        @pl.when(u > 0)
                        def _():
                            part = xh.at[q]
                            send(part, part, s_x.at[2, off - 1], r_x.at[2, off - 1], at_x(1)).wait_recv()

                        load_shard(xh, q)
                        for s in range(slots):
                            weigh(q * slots + s)

            @pl.loop(0, quads)
            def _(g):
                for i in range(4):
                    a = g * 4 + i
                    acc = jnp.zeros((RAYS, 128), F32)
                    for p in range(np_group):
                        first = (p * STRIDE + LEAD) // 8 - starts[p, o * ns + a]
                        acc = acc + pad[a, pl.ds(first, RAYS // 8)].reshape(RAYS, 128)
                    hi, lo = split(acc)
                    parts_hi[:, i * 128 : (i + 1) * 128] = hi
                    parts_lo[:, i * 128 : (i + 1) * 128] = lo
                if with_sums:
                    part = dot(parts_hi[...], pick[g]) + dot(parts_lo[...], pick[g])
                    zs[t, g] = part[:, :128]
                    sums[...] = jnp.where(g == 0, part[:, 128:], part[:, 128:] + sums[...])
                else:
                    zs[t, g] = dot(parts_hi[...], pick[0, :, 0:128]) + dot(parts_lo[...], pick[0, :, 0:128])

            if with_sums:
                zsum[t, :, 0:128] = jnp.transpose(sums[0:128])[0:ns]
                zsum[t, :, 128:RAYS] = jnp.transpose(sums[128:RAYS])[0:ns]
                zsum[t, :, RAYS:256] = jnp.ones((ns, 256 - RAYS), F32)

            @pl.when(t < nz - 1)
            def _():
                send(zs.at[t], zr.at[t], s_z.at[phase, t], r_z.at[phase, t], at_z(ahead(t))).start()
                if with_sums:
                    send(zsum.at[t], zrsum.at[t], s_sum.at[t], r_sum.at[t], at_z(ahead(t))).start()

    def end_forward(zs, zr, phase):
        for t in range(nz - 1):
            c = send(zs.at[t], zr.at[t], s_z.at[phase, t], r_z.at[phase, t], at_z(1 + t))
            c.wait_send()
            c.wait_recv()
            if phase == 0:
                c = send(zsum.at[t], zrsum.at[t], s_sum.at[t], r_sum.at[t], at_z(1 + t))
                c.wait_send()
                c.wait_recv()

    def total_rays(zs, zr, index):
        v = zs[nz - 1, index]
        for t in range(nz - 1):
            v = v + zr[t, index]
        return v * (1.0 / ROI)

    def spread(buf, phase):
        out = [
            send(buf.at[z], buf.at[z], s_z.at[phase, t - 1], r_z.at[phase, t - 1], at_z(t))
            for t in range(1, nz)
        ]
        for c in out:
            c.start()
        return out

    def backward(buf, pv, pr, phase):
        pv[...] = jnp.zeros_like(pv)

        @pl.loop(0, nz)
        def _(t):
            off = behind(t)
            o = lax.rem(z + nz - off, nz)

            @pl.when(t > 0)
            def _():
                send(buf.at[o], buf.at[o], s_z.at[phase, off - 1], r_z.at[phase, off - 1], at_z(1)).wait_recv()

            for g in range(quads):
                hi, lo = split(buf[o, g])
                wide = dot(hi, copy_out[...]) + dot(lo, copy_out[...])
                for i in range(4):
                    dr[g * 4 + i] = wide[:, i * 128 : (i + 1) * 128].reshape(RAYS // 8, 8, 128)

            rows = pl.ds(pl.multiple_of(o * (ns * TR), ns * TR), ns * TR)

            @pl.loop(0, nx)
            def _(u):
                q = lax.rem(x + ahead(u), nx)
                for g in range(quads):
                    for j in range(4):
                        a = g * 4 + j
                        out = None
                        for s in range(slots):
                            first = starts[q * slots + s, o * ns + a]
                            v = dr[a, pl.ds(first, TR // 8)].reshape(TR, 128)
                            out = v if s == 0 else jnp.where(lane == s, v, out)
                        tile[j * TR : (j + 1) * TR, :] = out
                    hi, lo = split(jnp.transpose(tile[...]))
                    for s in range(slots):
                        th[s, 0:32, g * 128 : (g + 1) * 128] = hi[s * 32 : (s + 1) * 32]
                        th[s, 32:64, g * 128 : (g + 1) * 128] = lo[s * 32 : (s + 1) * 32]
                for s in range(slots):
                    p = q * slots + s
                    both = dot(th[s], w_hi[p, rows, :])
                    low = dot(th[s, 0:32], w_lo[p, rows, :])
                    cols = slice(s * 256, (s + 1) * 256)
                    pv[u, :, cols] = pv[u, :, cols] + (both[:32] + (both[32:] + low))

                @pl.when((t == nz - 1) & (u < nx - 1))
                def _():
                    send(pv.at[u], pr.at[u], s_x.at[phase, u], r_x.at[phase, u], at_x(ahead(u))).start()

        for t in range(nx - 1):
            c = send(pv.at[t], pr.at[t], s_x.at[phase, t], r_x.at[phase, t], at_x(1 + t))
            c.wait_send()
            c.wait_recv()
        v = pv[nx - 1]
        for t in range(nx - 1):
            v = v + pr[t]
        return v * (RELAX / (ns * nz * nx))

    for c in loads:
        c.wait()
    modes = filter_forward(img, h_hi, h_lo, table, ping, pong)

    filter_back(modes, h_hi, h_lo, img, MID0, MID)
    for c in y_mid:
        c.start()

    xg[x] = x0[...]
    for c in x_out:
        c.wait()
    for q in range(nx):
        load_shard(xg, q)
    forward(zs0, zr0, 0)

    for base in (0, right0):

        @pl.loop(0, 3)
        def _(i, base=base):
            filter_back(modes, h_hi, h_lo, img, pl.multiple_of(base + i * 256, 128), 256)

        filter_back(modes, h_hi, h_lo, img, base + 768, 128)
    for c in y_side:
        c.start()
    ymid[slab] = img[own_rows, MID0 : MID0 + MID]
    res[slab] = img[own_rows, :]
    for c in y_mid:
        c.wait()
    for g in range(quads):
        block = ymid[g * 4 : (g + 1) * 4].reshape(128, MID)
        for h in range(MID // 128):
            yt[g, h * 128 : (h + 1) * 128, :] = jnp.transpose(block[:, h * 128 : (h + 1) * 128])
    end_forward(zs0, zr0, 0)
    total = zsum[nz - 1]
    for t in range(nz - 1):
        total = total + zrsum[t]
    inverse = 1.0 / jnp.maximum(total * (1.0 / ROI), ROW_FLOOR)
    inv_hi, inv_lo = split(jnp.concatenate([inverse, jnp.zeros_like(inverse)], axis=0))
    for g in range(quads):
        weight[g] = (dot_tn(inv_hi, copy_sum[g]) + dot_tn(inv_lo, copy_sum[g]))[:RAYS]
    for g in range(quads):
        dg[z, g] = (yt[g, SKIP : SKIP + RAYS, :] - total_rays(zs0, zr0, g)) * weight[g]
    d_out = spread(dg, 1)
    first = x0[...] + backward(dg, pv0, pr0, 1)
    for c in d_out:
        c.wait_send()
    xh[x] = first
    x_out = [
        send(xh.at[x], xh.at[x], s_x.at[2, t - 1], r_x.at[2, t - 1], at_x(t)) for t in range(1, nx)
    ]
    for c in x_out:
        c.start()
    forward(zs1, zr1, 2)
    for c in x_out:
        c.wait_send()
    end_forward(zs1, zr1, 2)
    for g in range(quads):
        diff = yt[g, SKIP : SKIP + RAYS, :] - total_rays(zs1, zr1, g)
        dh[z, g] = diff * weight[g]
        yt[g, SKIP : SKIP + RAYS, :] = diff
    d_out = spread(dh, 3)
    for g in range(quads):
        for h in range(MID // 128):
            turned = jnp.transpose(yt[g, h * 128 : (h + 1) * 128, :]).reshape(4, 32, 128)
            res[g * 4 : (g + 1) * 4, :, MID0 + h * 128 : MID0 + (h + 1) * 128] = turned
    last = first + backward(dh, pv1, pr1, 3)
    for s in range(slots):
        rec[:, s, :] = last[:, s * 256 : (s + 1) * 256]
    for c in d_out:
        c.wait_send()

    for c in y_side:
        c.wait()


def sirt(starts, offs, cs, image, volume, dims):
    height, width = image.shape
    table = filter_tables(height, width)
    anywhere = pl.BlockSpec(memory_space=pl.ANY)
    ns, nz, nx = dims
    np_group = 4 * nx
    na = ns * nz
    rows = na * TR
    quads = ns // 4
    dma = pltpu.SemaphoreType.DMA
    vm = pltpu.VMEM
    smem = pl.BlockSpec(memory_space=pltpu.SMEM)
    peers_z = max(nz - 1, 1)
    peers_x = max(nx - 1, 1)
    return pl.pallas_call(
        functools.partial(sirt_kernel, dims),
        out_shape=(
            jax.ShapeDtypeStruct((ns, 32, BAND), F32),
            jax.ShapeDtypeStruct(volume.shape, F32),
        ),
        in_specs=[smem] * 3 + [anywhere, pl.BlockSpec(memory_space=pltpu.VMEM), anywhere],
        out_specs=(pl.BlockSpec(memory_space=pltpu.VMEM), pl.BlockSpec(memory_space=pltpu.VMEM)),
        scratch_shapes=[
            vm((32, 1024), F32),
            vm((height, width), F32),
            vm((height // 128, width + 2 * HALO, 128), F32),
            vm((height // 128, width + 2 * HALO, 128), F32),
            vm((height, height), BF16),
            vm((height, height), BF16),
            vm((RAYS, 512), BF16),
            vm((RAYS, 512), BF16),
            vm((quads, 512, 256), BF16),
            vm((128, 512), BF16),
            vm((quads, 16, 128), BF16),
            vm((RAYS, 128), F32),
            vm((np_group, rows, 256), BF16),
            vm((np_group, rows, 256), BF16),
            vm((np_group, 128, 256), BF16),
            vm((ns, (np_group * STRIDE + LEAD) // 8, 8, 128), F32),
            vm((nx, 32, 1024), F32),
            vm((nx, 32, 1024), F32),
            vm((nz, quads, RAYS, 128), F32),
            vm((peers_z, quads, RAYS, 128), F32),
            vm((nz, quads, RAYS, 128), F32),
            vm((peers_z, quads, RAYS, 128), F32),
            vm((nz, quads, RAYS, 128), F32),
            vm((nz, quads, RAYS, 128), F32),
            vm((ns, RAYS // 8, 8, 128), F32),
            vm((128, 128), F32),
            vm((4, 64, ns * TR), BF16),
            vm((nx, 32, 1024), F32),
            vm((peers_x, 32, 1024), F32),
            vm((nx, 32, 1024), F32),
            vm((peers_x, 32, 1024), F32),
            vm((ns, 32, MID), F32),
            vm((quads, MID, 128), F32),
            vm((quads, RAYS, 128), F32),
            vm((nz, ns, 256), F32),
            vm((peers_z, ns, 256), F32),
            dma((peers_z,)),
            dma((peers_z,)),
            dma((ns - 1,)),
            dma((ns - 1,)),
            dma((ns - 1,)),
            dma((ns - 1,)),
            dma((ns - 1,)),
            dma((ns - 1,)),
            dma((4, peers_x)),
            dma((4, peers_x)),
            dma((4, peers_z)),
            dma((4, peers_z)),
            dma((8,)),
        ],
        compiler_params=pltpu.CompilerParams(
            collective_id=0, has_side_effects=True, vmem_limit_bytes=50 << 20
        ),
        name="sirt",
    )(starts, offs, cs, image, jnp.asarray(table), volume)


def tables_kernel(dims, angles, ids, starts, offs, cs):
    ns, nz, nx = dims
    ray = lax.axis_index("ray")
    z = ray // nx
    x = lax.rem(ray, nx)
    shape = (4 * nx, 128)
    row = lax.broadcasted_iota(jnp.int32, shape, 0)
    lane = lax.broadcasted_iota(jnp.int32, shape, 1)
    theta = jnp.zeros(shape, F32)
    for a in range(ns * nz):
        theta = jnp.where(lane == a, angles[a % ns, a // ns * nx + x], theta)
    patch = jnp.zeros(shape, jnp.int32)
    for p in range(4 * nx):
        patch = jnp.where(row == p, ids[z * 4 * nx + p], patch)
    cosine = jnp.cos(theta)
    sine = jnp.sin(theta)
    centre_x = (patch // PGRID).astype(F32) * 16.0 + 7.5 - HALF_ROI
    centre_y = (patch % PGRID).astype(F32) * 16.0 + 7.5 - HALF_ROI
    centre = HALF_BAND + centre_x * cosine + centre_y * sine
    first = jnp.floor(centre - 11.61).astype(jnp.int32) + 1
    start = first // 8
    starts[...] = start - RAY0 // 8
    offs[...] = (start * 8).astype(F32) - centre
    cs[0:8, :] = cosine[0:8]
    cs[8:16, :] = sine[0:8]


def tile_tables(angles, vol_list, dims):
    shape = (4 * dims[2], 128)
    return pl.pallas_call(
        functools.partial(tables_kernel, dims),
        out_shape=(
            jax.ShapeDtypeStruct(shape, jnp.int32),
            jax.ShapeDtypeStruct(shape, F32),
            jax.ShapeDtypeStruct((16, 128), F32),
        ),
        in_specs=[pl.BlockSpec(memory_space=pltpu.SMEM)] * 2,
        out_specs=(pl.BlockSpec(memory_space=pltpu.VMEM),) * 3,
        compiler_params=pltpu.CompilerParams(vmem_limit_bytes=4 << 20),
        name="tile_tables",
    )(angles, vol_list)


def local(dims, intensity, angles, volume, vol_list):
    ns, nz, nx = dims
    height = intensity.shape[2]
    starts, offs, cs = tile_tables(angles, vol_list, dims)
    res, rec = sirt(starts, offs, cs, intensity.reshape(height, BAND), volume, dims)
    return rec, res[:, None]


def make(mesh, dims):
    placed = (P("slab", "ray", None, None), P(), P("slab", "ray", None), P())
    return jax.shard_map(
        functools.partial(local, dims),
        mesh=mesh,
        in_specs=placed,
        out_specs=(P("slab", "ray", None), P(None, "ray", "slab", None)),
        check_vma=False,
    )


def solution(mesh):
    return make(mesh, (mesh.shape["slab"], 4, mesh.shape["ray"] // 4))
```

```python
import functools

import jax
import jax.numpy as jnp
import numpy as np
from jax import lax
from jax.experimental import pallas as pl
from jax.experimental.pallas import tpu as pltpu
from jax.sharding import PartitionSpec as P

BAND = 2048
PGRID = 8
ROI = 128
HALF_ROI = (ROI - 1) / 2.0
HALF_BAND = (BAND - 1) / 2.0
STRENGTH = 10.0
RELAX = 1.8
ROW_FLOOR = 0.25
MESH = pl.DeviceIdType.MESH

TR = 32
MID0 = 896
MID = 256
RAY0 = 932
RAYS = 184
SKIP = RAY0 - MID0
STRIDE = RAYS
LEAD = RAYS - TR
F32 = jnp.float32
BF16 = jnp.bfloat16
HALO = 64


def dot(a, b):
    return lax.dot_general(a, b, (((1,), (0,)), ((), ())), preferred_element_type=F32)


def dot_nt(a, b):
    return lax.dot_general(a, b, (((1,), (1,)), ((), ())), preferred_element_type=F32)


def dot_tn(a, b):
    return lax.dot_general(a, b, (((0,), (0,)), ((), ())), preferred_element_type=F32)


def split(v):
    hi = v.astype(BF16)
    return hi, (v - hi.astype(F32)).astype(BF16)


def filter_tables(height, width):
    m = np.arange(height)
    ang = 2.0 * np.pi * (np.outer(m, m) % height) / height
    had = (np.cos(ang) + np.sin(ang)) / np.sqrt(height)
    beta = 1.0 + STRENGTH * (2.0 - 2.0 * np.cos(2.0 * np.pi * m / height)) + 2.0 * STRENGTH
    half = beta / (2.0 * STRENGTH)
    root = half - np.sqrt(half * half - 1.0)
    scale = root / STRENGTH / (1.0 - root**width) ** 2
    steps = int(np.log2(width))
    table = np.zeros((16, height))
    power = root
    for k in range(steps):
        table[k] = power / (1.0 + power * power)
        scale = scale * (1.0 + power * power)
        power = power * power
    table[15] = scale
    return np.concatenate([had, table]).astype(np.float32)


def filter_forward(img, h_hi, h_lo, table, ping, pong):
    height, width = img.shape
    chunk = 256
    halves = height // 128

    @pl.loop(0, width // chunk)
    def _(c):
        cols = pl.ds(pl.multiple_of(c * chunk, chunk), chunk)
        rows = pl.ds(pl.multiple_of(HALO + c * chunk, 8), chunk)
        v_hi, v_lo = split(jnp.transpose(1.0 - img[:, cols]))
        v = dot(v_hi, h_hi[...]) + (dot(v_lo, h_hi[...]) + dot(v_hi, h_lo[...]))
        for h in range(halves):
            ping[h, rows, :] = v[:, h * 128 : (h + 1) * 128]

    def row(k, h):
        return jnp.broadcast_to(table[k : k + 1, h * 128 : (h + 1) * 128], (8, 128))

    source, target = ping, pong
    step, k = 1, 0
    while step <= HALO:
        for h in range(halves):
            source[h, 0:HALO, :] = source[h, width : width + HALO, :]
            source[h, width + HALO : width + 2 * HALO, :] = source[h, HALO : 2 * HALO, :]
            rate = row(k, h)

            @pl.loop(0, width // 128)
            def _(b, h=h, step=step, source=source, target=target, rate=rate):
                for i in range(16):
                    at = b * 128 + HALO + 8 * i
                    here = source[h, pl.ds(at, 8), :]
                    near = source[h, pl.ds(at - step, 8), :] + source[h, pl.ds(at + step, 8), :]
                    target[h, pl.ds(at, 8), :] = here + rate * near

        source, target = target, source
        step *= 2
        k += 1

    for h in range(halves):
        rates = [row(j, h) for j in range(k, k + 4)]
        scale = row(15, h)

        @pl.loop(0, 16)
        def _(i, h=h, rates=rates, scale=scale):
            v = [source[h, pl.ds(HALO + b * 128 + 8 * i, 8), :] for b in range(16)]
            for j, rate in zip((1, 2, 4, 8), rates):
                v = [v[b] + rate * (v[b - j] + v[(b + j) % 16]) for b in range(16)]
            for b in range(16):
                target[h, pl.ds(HALO + b * 128 + 8 * i, 8), :] = v[b] * scale

    return target


def filter_back(modes, h_hi, h_lo, out, first, count):
    rows = pl.ds(HALO + first, count)
    v = jnp.concatenate([modes[h, rows, :] for h in range(out.shape[0] // 128)], axis=1)
    v_hi, v_lo = split(v)
    v = dot_nt(h_hi[...], v_hi) + (dot_nt(h_hi[...], v_lo) + dot_nt(h_lo[...], v_hi))
    out[:, pl.ds(first, count)] = -jnp.log(1.0 - v)


def sirt_kernel(
    dims,
    starts,
    offs,
    cs,
    image,
    table_in,
    volume,
    res,
    rec,
    x0,
    img,
    ping,
    pong,
    h_hi,
    h_lo,
    parts_hi,
    parts_lo,
    pick,
    copy_out,
    copy_sum,
    sums,
    w_hi,
    w_lo,
    xb,
    pad,
    xg,
    xh,
    zs0,
    zr0,
    zs1,
    zr1,
    dg,
    dh,
    dr,
    tile,
    th,
    pv0,
    pr0,
    pv1,
    pr1,
    ymid,
    yt,
    weight,
    zsum,
    zrsum,
    s_sum,
    r_sum,
    s_mid,
    r_mid,
    s_left,
    r_left,
    s_right,
    r_right,
    s_x,
    r_x,
    s_z,
    r_z,
    s_loc,
):
    ns, nz, nx = dims
    slots = 4
    np_group = slots * nx
    na = ns * nz
    quads = ns // 4
    right0 = MID0 + MID
    rightn = BAND - right0
    slab = lax.axis_index("slab")
    ray = lax.axis_index("ray")
    z = ray // nx
    x = lax.rem(ray, nx)

    def at_slab(t):
        return {"slab": lax.rem(slab + t, ns), "ray": ray}

    def at_z(t):
        return {"slab": slab, "ray": lax.rem(z + t, nz) * nx + x}

    def at_x(t):
        return {"slab": slab, "ray": z * nx + lax.rem(x + t, nx)}

    loads = [
        pltpu.make_async_copy(image, img, s_loc.at[7]),
    ]
    x_loads = [
        pltpu.make_async_copy(volume.at[:, s, :], x0.at[:, pl.ds(s * 256, 256)], s_loc.at[s])
        for s in range(slots)
    ]
    for c in x_loads + loads:
        c.start()
    barrier = pltpu.get_barrier_semaphore()
    for t in range(1, nx):
        pl.semaphore_signal(barrier, inc=1, device_id=at_x(t), device_id_type=MESH)
    for t in range(1, nz):
        pl.semaphore_signal(barrier, inc=1, device_id=at_z(t), device_id_type=MESH)
    for t in range(1, ns):
        pl.semaphore_signal(barrier, inc=1, device_id=at_slab(t), device_id_type=MESH)
    pl.semaphore_wait(barrier, nx + nz + ns - 3)

    def send(src, dst, ssem, rsem, device):
        return pltpu.make_async_remote_copy(
            src_ref=src, dst_ref=dst, send_sem=ssem, recv_sem=rsem, device_id=device, device_id_type=MESH
        )

    for c in x_loads:
        c.wait()
    x_out = [
        send(x0, xg.at[x], s_x.at[0, t - 1], r_x.at[0, t - 1], at_x(t)) for t in range(1, nx)
    ]
    for c in x_out:
        c.start()
    y_mid, y_side = [], []
    own_rows = pl.ds(pl.multiple_of(slab * 32, 32), 32)
    for t in range(1, ns):
        to = pl.ds(pl.multiple_of(lax.rem(slab + t, ns) * 32, 32), 32)
        y_mid.append(
            send(
                img.at[to, pl.ds(MID0, MID)], ymid.at[slab], s_mid.at[t - 1], r_mid.at[t - 1], at_slab(t)
            )
        )
        y_side.append(
            send(
                img.at[to, pl.ds(0, MID0)],
                res.at[slab, :, pl.ds(0, MID0)],
                s_left.at[t - 1],
                r_left.at[t - 1],
                at_slab(t),
            )
        )
        y_side.append(
            send(
                img.at[to, pl.ds(right0, rightn)],
                res.at[slab, :, pl.ds(right0, rightn)],
                s_right.at[t - 1],
                r_right.at[t - 1],
                at_slab(t),
            )
        )

    height = img.shape[0]
    h_hi[...], h_lo[...] = split(table_in[0:height, :])
    table = table_in.at[pl.ds(height, 16), :]

    vox = lax.broadcasted_iota(jnp.int32, (1, 256), 1)
    dx = (vox // 16).astype(F32) - 7.5
    dy = lax.rem(vox, 16).astype(F32) - 7.5
    lane_ray = lax.broadcasted_iota(jnp.int32, (TR, 256), 0).astype(F32)

    @pl.loop(0, na)
    def _(a):
        base = lane_ray - (dx * cs[0, a] + dy * cs[8, a])
        rows = pl.ds(pl.multiple_of(a * TR, TR), TR)

        @pl.loop(0, np_group)
        def _(p):
            hat = jnp.maximum(0.0, 1.0 - jnp.abs(base + offs[p, a]))
            hi, lo = split(hat)
            w_hi[p, rows, :] = hi
            w_lo[p, rows, :] = lo

    @pl.loop(0, ns)
    def _(a):
        for p in range(np_group):
            pad[a, pl.ds(p * STRIDE // 8, LEAD // 8)] = jnp.zeros((LEAD // 8, 8, 128), F32)
        pad[a, pl.ds(np_group * STRIDE // 8, LEAD // 8)] = jnp.zeros((LEAD // 8, 8, 128), F32)

    @pl.loop(0, np_group)
    def _(p):
        xb[p, 64:96, :] = jnp.ones((32, 256), BF16)
        xb[p, 96:128, :] = jnp.zeros((32, 256), BF16)

    lane = lax.broadcasted_iota(jnp.int32, (1, 128), 1) // 32

    def one_hot(shape, test):
        r = lax.broadcasted_iota(jnp.int32, shape, 0)
        c = lax.broadcasted_iota(jnp.int32, shape, 1)
        return jnp.where(test(r, c), 1.0, 0.0).astype(BF16)

    for g in range(quads):
        pick[g, :, 0:128] = one_hot(
            (512, 128), lambda r, c: (r % 128 < 64) & (r % 32 == c % 32) & (r // 128 == c // 32)
        )
        pick[g, :, 128:256] = one_hot(
            (512, 128), lambda r, c, g=g: (r % 128 == 64) & (g * 4 + r // 128 == c)
        )
        copy_sum[g] = one_hot((16, 128), lambda r, c, g=g: r == g * 4 + c // 32)
    copy_out[...] = one_hot((128, 512), lambda r, c: (r // 32 == c // 128) & (r % 32 == c % 32))

    def load_shard(source, q, copies):
        for s in range(slots):
            hi, lo = split(source[q, :, pl.ds(s * 256, 256)])
            for k in range(copies):
                xb[q * slots + s, k * 32 : (k + 1) * 32, :] = hi
                low = (k + copies) * 32
                xb[q * slots + s, low : low + 32, :] = lo

    def ahead(t):
        return 2 - t + 3 * (t // 2) + 2 * (t // 3)

    def behind(t):
        return t + t // 2 - 2 * (t // 3)

    def forward(zs, zr, phase):
        with_sums = phase == 0

        @pl.loop(0, nz)
        def _(t):
            o = lax.rem(z + ahead(t), nz)
            rows = pl.ds(pl.multiple_of(o * (ns * TR), ns * TR), ns * TR)

            def weigh(p):
                wide = xb[p, 0:128] if with_sums else xb[p]
                part = dot_nt(w_hi[p, rows, :], wide) + dot_nt(w_lo[p, rows, :], wide)
                if not with_sums:
                    part = part[:, :128] + part[:, 128:]
                at = pl.ds(p * (STRIDE // 8) + LEAD // 8, TR // 8)
                for a in range(ns):
                    pad[a, at] = part[a * TR : (a + 1) * TR].reshape(TR // 8, 8, 128)

            def weigh_all():
                @pl.loop(0, np_group, unroll=16 if with_sums else 8)
                def _(p):
                    weigh(p)

            if phase == 0:
                weigh_all()
            else:
                pl.when(t > 0)(weigh_all)

                @pl.when(t == 0)
                def _():
                    @pl.loop(0, nx)
                    def _(u):
                        off = behind(u)
                        q = lax.rem(x + nx - off, nx)

                        @pl.when(u > 0)
                        def _():
                            part = xh.at[q]
                            send(part, part, s_x.at[2, off - 1], r_x.at[2, off - 1], at_x(1)).wait_recv()

                        load_shard(xh, q, 4)
                        for s in range(slots):
                            weigh(q * slots + s)

            @pl.loop(0, quads)
            def _(g):
                packed = jnp.zeros((RAYS, 128), F32)
                for i in range(4):
                    a = g * 4 + i
                    acc = jnp.zeros((RAYS, 128), F32)
                    for p in range(np_group):
                        first = (p * STRIDE + LEAD) // 8 - starts[p, o * ns + a]
                        acc = acc + pad[a, pl.ds(first, RAYS // 8)].reshape(RAYS, 128)
                    if with_sums:
                        hi, lo = split(acc)
                        parts_hi[0:RAYS, i * 128 : (i + 1) * 128] = hi
                        parts_lo[0:RAYS, i * 128 : (i + 1) * 128] = lo
                    else:
                        packed = jnp.where(lane == i, acc, packed)
                if with_sums:
                    part = dot(parts_hi[0:RAYS], pick[g]) + dot(parts_lo[0:RAYS], pick[g])
                    zs[t, g] = part[:, :128]
                    sums[...] = jnp.where(g == 0, part[:, 128:], part[:, 128:] + sums[...])
                else:
                    zs[t, g] = packed

            if with_sums:
                zsum[t, :, 0:128] = jnp.transpose(sums[0:128])[0:ns]
                zsum[t, :, 128:RAYS] = jnp.transpose(sums[128:RAYS])[0:ns]
                zsum[t, :, RAYS:256] = jnp.ones((ns, 256 - RAYS), F32)

            @pl.when(t < nz - 1)
            def _():
                send(zs.at[t], zr.at[t], s_z.at[phase, t], r_z.at[phase, t], at_z(ahead(t))).start()
                if with_sums:
                    send(zsum.at[t], zrsum.at[t], s_sum.at[t], r_sum.at[t], at_z(ahead(t))).start()

    def end_forward(zs, zr, phase):
        for t in range(nz - 1):
            c = send(zs.at[t], zr.at[t], s_z.at[phase, t], r_z.at[phase, t], at_z(1 + t))
            c.wait_send()
            c.wait_recv()
            if phase == 0:
                c = send(zsum.at[t], zrsum.at[t], s_sum.at[t], r_sum.at[t], at_z(1 + t))
                c.wait_send()
                c.wait_recv()

    def total_rays(zs, zr, index):
        v = zs[nz - 1, index]
        for t in range(nz - 1):
            v = v + zr[t, index]
        return v * (1.0 / ROI)

    def spread(buf, phase):
        out = [
            send(buf.at[z], buf.at[z], s_z.at[phase, t - 1], r_z.at[phase, t - 1], at_z(t))
            for t in range(1, nz)
        ]
        for c in out:
            c.start()
        return out

    def backward(buf, pv, pr, phase):
        pv[...] = jnp.zeros_like(pv)

        @pl.loop(0, nz)
        def _(t):
            off = behind(t)
            o = lax.rem(z + nz - off, nz)

            @pl.when(t > 0)
            def _():
                send(buf.at[o], buf.at[o], s_z.at[phase, off - 1], r_z.at[phase, off - 1], at_z(1)).wait_recv()

            for g in range(quads):
                hi, lo = split(buf[o, g])
                wide = dot(hi, copy_out[...]) + dot(lo, copy_out[...])
                for i in range(4):
                    dr[g * 4 + i] = wide[:, i * 128 : (i + 1) * 128].reshape(RAYS // 8, 8, 128)

            rows = pl.ds(pl.multiple_of(o * (ns * TR), ns * TR), ns * TR)

            @pl.loop(0, nx)
            def _(u):
                q = lax.rem(x + ahead(u), nx)
                for g in range(quads):
                    for j in range(4):
                        a = g * 4 + j
                        out = None
                        for s in range(slots):
                            first = starts[q * slots + s, o * ns + a]
                            v = dr[a, pl.ds(first, TR // 8)].reshape(TR, 128)
                            out = v if s == 0 else jnp.where(lane == s, v, out)
                        tile[j * TR : (j + 1) * TR, :] = out
                    hi, lo = split(jnp.transpose(tile[...]))
                    for s in range(slots):
                        th[s, 0:32, g * 128 : (g + 1) * 128] = hi[s * 32 : (s + 1) * 32]
                        th[s, 32:64, g * 128 : (g + 1) * 128] = lo[s * 32 : (s + 1) * 32]
                for s in range(slots):
                    p = q * slots + s
                    both = dot(th[s], w_hi[p, rows, :])
                    low = dot(th[s, 0:32], w_lo[p, rows, :])
                    cols = slice(s * 256, (s + 1) * 256)
                    pv[u, :, cols] = pv[u, :, cols] + (both[:32] + (both[32:] + low))

                @pl.when((t == nz - 1) & (u < nx - 1))
                def _():
                    send(pv.at[u], pr.at[u], s_x.at[phase, u], r_x.at[phase, u], at_x(ahead(u))).start()

        for t in range(nx - 1):
            c = send(pv.at[t], pr.at[t], s_x.at[phase, t], r_x.at[phase, t], at_x(1 + t))
            c.wait_send()
            c.wait_recv()
        v = pv[nx - 1]
        for t in range(nx - 1):
            v = v + pr[t]
        return v * (RELAX / (ns * nz * nx))

    for c in loads:
        c.wait()
    modes = filter_forward(img, h_hi, h_lo, table, ping, pong)

    filter_back(modes, h_hi, h_lo, img, MID0, MID)
    for c in y_mid:
        c.start()

    xg[x] = x0[...]
    for c in x_out:
        c.wait()
    for q in range(nx):
        load_shard(xg, q, 1)
    forward(zs0, zr0, 0)

    for base in (0, right0):

        @pl.loop(0, 3)
        def _(i, base=base):
            filter_back(modes, h_hi, h_lo, img, pl.multiple_of(base + i * 256, 128), 256)

        filter_back(modes, h_hi, h_lo, img, base + 768, 128)
    for c in y_side:
        c.start()
    ymid[slab] = img[own_rows, MID0 : MID0 + MID]
    res[slab] = img[own_rows, :]
    for c in y_mid:
        c.wait()
    for g in range(quads):
        block = ymid[g * 4 : (g + 1) * 4].reshape(128, MID)
        for h in range(MID // 128):
            yt[g, h * 128 : (h + 1) * 128, :] = jnp.transpose(block[:, h * 128 : (h + 1) * 128])
    end_forward(zs0, zr0, 0)
    total = zsum[nz - 1]
    for t in range(nz - 1):
        total = total + zrsum[t]
    inverse = 1.0 / jnp.maximum(total * (1.0 / ROI), ROW_FLOOR)
    inv_hi, inv_lo = split(jnp.concatenate([inverse, jnp.zeros_like(inverse)], axis=0))
    for g in range(quads):
        weight[g] = (dot_tn(inv_hi, copy_sum[g]) + dot_tn(inv_lo, copy_sum[g]))[:RAYS]
    for g in range(quads):
        dg[z, g] = (yt[g, SKIP : SKIP + RAYS, :] - total_rays(zs0, zr0, g)) * weight[g]
    d_out = spread(dg, 1)
    first = x0[...] + backward(dg, pv0, pr0, 1)
    for c in d_out:
        c.wait_send()
    xh[x] = first
    x_out = [
        send(xh.at[x], xh.at[x], s_x.at[2, t - 1], r_x.at[2, t - 1], at_x(t)) for t in range(1, nx)
    ]
    for c in x_out:
        c.start()
    forward(zs1, zr1, 2)
    for c in x_out:
        c.wait_send()
    end_forward(zs1, zr1, 2)
    for g in range(quads):
        diff = yt[g, SKIP : SKIP + RAYS, :] - total_rays(zs1, zr1, g)
        dh[z, g] = diff * weight[g]
        yt[g, SKIP : SKIP + RAYS, :] = diff
    d_out = spread(dh, 3)
    for g in range(quads):
        for h in range(MID // 128):
            turned = jnp.transpose(yt[g, h * 128 : (h + 1) * 128, :]).reshape(4, 32, 128)
            res[g * 4 : (g + 1) * 4, :, MID0 + h * 128 : MID0 + (h + 1) * 128] = turned
    last = first + backward(dh, pv1, pr1, 3)
    for s in range(slots):
        rec[:, s, :] = last[:, s * 256 : (s + 1) * 256]
    for c in d_out:
        c.wait_send()

    for c in y_side:
        c.wait()


def sirt(starts, offs, cs, image, volume, dims):
    height, width = image.shape
    table = filter_tables(height, width)
    anywhere = pl.BlockSpec(memory_space=pl.ANY)
    ns, nz, nx = dims
    np_group = 4 * nx
    na = ns * nz
    rows = na * TR
    quads = ns // 4
    dma = pltpu.SemaphoreType.DMA
    vm = pltpu.VMEM
    smem = pl.BlockSpec(memory_space=pltpu.SMEM)
    peers_z = max(nz - 1, 1)
    peers_x = max(nx - 1, 1)
    return pl.pallas_call(
        functools.partial(sirt_kernel, dims),
        out_shape=(
            jax.ShapeDtypeStruct((ns, 32, BAND), F32),
            jax.ShapeDtypeStruct(volume.shape, F32),
        ),
        in_specs=[smem] * 3 + [anywhere, pl.BlockSpec(memory_space=pltpu.VMEM), anywhere],
        out_specs=(pl.BlockSpec(memory_space=pltpu.VMEM), pl.BlockSpec(memory_space=pltpu.VMEM)),
        scratch_shapes=[
            vm((32, 1024), F32),
            vm((height, width), F32),
            vm((height // 128, width + 2 * HALO, 128), F32),
            vm((height // 128, width + 2 * HALO, 128), F32),
            vm((height, height), BF16),
            vm((height, height), BF16),
            vm((192, 512), BF16),
            vm((192, 512), BF16),
            vm((quads, 512, 256), BF16),
            vm((128, 512), BF16),
            vm((quads, 16, 128), BF16),
            vm((RAYS, 128), F32),
            vm((np_group, rows, 256), BF16),
            vm((np_group, rows, 256), BF16),
            vm((np_group, 256, 256), BF16),
            vm((ns, (np_group * STRIDE + LEAD) // 8, 8, 128), F32),
            vm((nx, 32, 1024), F32),
            vm((nx, 32, 1024), F32),
            vm((nz, quads, RAYS, 128), F32),
            vm((peers_z, quads, RAYS, 128), F32),
            vm((nz, quads, RAYS, 128), F32),
            vm((peers_z, quads, RAYS, 128), F32),
            vm((nz, quads, RAYS, 128), F32),
            vm((nz, quads, RAYS, 128), F32),
            vm((ns, RAYS // 8, 8, 128), F32),
            vm((128, 128), F32),
            vm((4, 64, ns * TR), BF16),
            vm((nx, 32, 1024), F32),
            vm((peers_x, 32, 1024), F32),
            vm((nx, 32, 1024), F32),
            vm((peers_x, 32, 1024), F32),
            vm((ns, 32, MID), F32),
            vm((quads, MID, 128), F32),
            vm((quads, RAYS, 128), F32),
            vm((nz, ns, 256), F32),
            vm((peers_z, ns, 256), F32),
            dma((peers_z,)),
            dma((peers_z,)),
            dma((ns - 1,)),
            dma((ns - 1,)),
            dma((ns - 1,)),
            dma((ns - 1,)),
            dma((ns - 1,)),
            dma((ns - 1,)),
            dma((4, peers_x)),
            dma((4, peers_x)),
            dma((4, peers_z)),
            dma((4, peers_z)),
            dma((8,)),
        ],
        compiler_params=pltpu.CompilerParams(
            collective_id=0, has_side_effects=True, vmem_limit_bytes=51 << 20
        ),
        name="sirt",
    )(starts, offs, cs, image, jnp.asarray(table), volume)


def tables_kernel(dims, angles, ids, starts, offs, cs):
    ns, nz, nx = dims
    ray = lax.axis_index("ray")
    z = ray // nx
    x = lax.rem(ray, nx)
    shape = (4 * nx, 128)
    row = lax.broadcasted_iota(jnp.int32, shape, 0)
    lane = lax.broadcasted_iota(jnp.int32, shape, 1)
    theta = jnp.zeros(shape, F32)
    for a in range(ns * nz):
        theta = jnp.where(lane == a, angles[a % ns, a // ns * nx + x], theta)
    patch = jnp.zeros(shape, jnp.int32)
    for p in range(4 * nx):
        patch = jnp.where(row == p, ids[z * 4 * nx + p], patch)
    cosine = jnp.cos(theta)
    sine = jnp.sin(theta)
    centre_x = (patch // PGRID).astype(F32) * 16.0 + 7.5 - HALF_ROI
    centre_y = (patch % PGRID).astype(F32) * 16.0 + 7.5 - HALF_ROI
    centre = HALF_BAND + centre_x * cosine + centre_y * sine
    first = jnp.floor(centre - 11.61).astype(jnp.int32) + 1
    start = jnp.minimum((first - RAY0) // 8, (RAYS - TR) // 8)
    starts[...] = start
    offs[...] = (start * 8 + RAY0).astype(F32) - centre
    cs[0:8, :] = cosine[0:8]
    cs[8:16, :] = sine[0:8]


def tile_tables(angles, vol_list, dims):
    shape = (4 * dims[2], 128)
    return pl.pallas_call(
        functools.partial(tables_kernel, dims),
        out_shape=(
            jax.ShapeDtypeStruct(shape, jnp.int32),
            jax.ShapeDtypeStruct(shape, F32),
            jax.ShapeDtypeStruct((16, 128), F32),
        ),
        in_specs=[pl.BlockSpec(memory_space=pltpu.SMEM)] * 2,
        out_specs=(pl.BlockSpec(memory_space=pltpu.VMEM),) * 3,
        compiler_params=pltpu.CompilerParams(vmem_limit_bytes=4 << 20),
        name="tile_tables",
    )(angles, vol_list)


def local(dims, intensity, angles, volume, vol_list):
    ns, nz, nx = dims
    height = intensity.shape[2]
    starts, offs, cs = tile_tables(angles, vol_list, dims)
    res, rec = sirt(starts, offs, cs, intensity.reshape(height, BAND), volume, dims)
    return rec, res[:, None]


def make(mesh, dims):
    placed = (P("slab", "ray", None, None), P(), P("slab", "ray", None), P())
    return jax.shard_map(
        functools.partial(local, dims),
        mesh=mesh,
        in_specs=placed,
        out_specs=(P("slab", "ray", None), P(None, "ray", "slab", None)),
        check_vma=False,
    )


def solution(mesh):
    return make(mesh, (mesh.shape["slab"], 4, mesh.shape["ray"] // 4))
```

```python
import functools

import jax
import jax.numpy as jnp
import numpy as np
from jax import lax
from jax.experimental import pallas as pl
from jax.experimental.pallas import tpu as pltpu
from jax.sharding import PartitionSpec as P

BAND = 2048
PGRID = 8
ROI = 128
HALF_ROI = (ROI - 1) / 2.0
HALF_BAND = (BAND - 1) / 2.0
STRENGTH = 10.0
RELAX = 1.8
ROW_FLOOR = 0.25
MESH = pl.DeviceIdType.MESH

TR = 32
MID0 = 896
MID = 256
RAY0 = 932
RAYS = 184
SKIP = RAY0 - MID0
STRIDE = RAYS
LEAD = RAYS - TR
F32 = jnp.float32
BF16 = jnp.bfloat16
HALO = 64


def dot(a, b):
    return lax.dot_general(a, b, (((1,), (0,)), ((), ())), preferred_element_type=F32)


def dot_nt(a, b):
    return lax.dot_general(a, b, (((1,), (1,)), ((), ())), preferred_element_type=F32)


def dot_tn(a, b):
    return lax.dot_general(a, b, (((0,), (0,)), ((), ())), preferred_element_type=F32)


def split(v):
    hi = v.astype(BF16)
    return hi, (v - hi.astype(F32)).astype(BF16)


def filter_tables(height, width):
    m = np.arange(height)
    ang = 2.0 * np.pi * (np.outer(m, m) % height) / height
    had = (np.cos(ang) + np.sin(ang)) / np.sqrt(height)
    beta = 1.0 + STRENGTH * (2.0 - 2.0 * np.cos(2.0 * np.pi * m / height)) + 2.0 * STRENGTH
    half = beta / (2.0 * STRENGTH)
    root = half - np.sqrt(half * half - 1.0)
    scale = root / STRENGTH / (1.0 - root**width) ** 2
    steps = int(np.log2(width))
    table = np.zeros((16, height))
    power = root
    for k in range(steps):
        table[k] = power / (1.0 + power * power)
        scale = scale * (1.0 + power * power)
        power = power * power
    table[15] = scale
    return np.concatenate([had, table]).astype(np.float32)


def filter_forward(img, h_hi, h_lo, table, ping, pong):
    height, width = img.shape
    chunk = 256
    halves = height // 128

    @pl.loop(0, width // chunk)
    def _(c):
        cols = pl.ds(pl.multiple_of(c * chunk, chunk), chunk)
        rows = pl.ds(pl.multiple_of(HALO + c * chunk, 8), chunk)
        v_hi, v_lo = split(jnp.transpose(1.0 - img[:, cols]))
        v = dot(v_hi, h_hi[...]) + (dot(v_lo, h_hi[...]) + dot(v_hi, h_lo[...]))
        for h in range(halves):
            ping[h, rows, :] = v[:, h * 128 : (h + 1) * 128]

    def row(k, h):
        return jnp.broadcast_to(table[k : k + 1, h * 128 : (h + 1) * 128], (8, 128))

    source, target = ping, pong
    step, k = 1, 0
    while step <= HALO:
        for h in range(halves):
            source[h, 0:HALO, :] = source[h, width : width + HALO, :]
            source[h, width + HALO : width + 2 * HALO, :] = source[h, HALO : 2 * HALO, :]
            rate = row(k, h)

            @pl.loop(0, width // 128)
            def _(b, h=h, step=step, source=source, target=target, rate=rate):
                for i in range(16):
                    at = b * 128 + HALO + 8 * i
                    here = source[h, pl.ds(at, 8), :]
                    near = source[h, pl.ds(at - step, 8), :] + source[h, pl.ds(at + step, 8), :]
                    target[h, pl.ds(at, 8), :] = here + rate * near

        source, target = target, source
        step *= 2
        k += 1

    for h in range(halves):
        rates = [row(j, h) for j in range(k, k + 4)]
        scale = row(15, h)

        @pl.loop(0, 16)
        def _(i, h=h, rates=rates, scale=scale):
            v = [source[h, pl.ds(HALO + b * 128 + 8 * i, 8), :] for b in range(16)]
            for j, rate in zip((1, 2, 4, 8), rates):
                v = [v[b] + rate * (v[b - j] + v[(b + j) % 16]) for b in range(16)]
            for b in range(16):
                target[h, pl.ds(HALO + b * 128 + 8 * i, 8), :] = v[b] * scale

    return target


def filter_back(modes, h_hi, h_lo, out, first, count):
    rows = pl.ds(HALO + first, count)
    v = jnp.concatenate([modes[h, rows, :] for h in range(out.shape[0] // 128)], axis=1)
    v_hi, v_lo = split(v)
    v = dot_nt(h_hi[...], v_hi) + (dot_nt(h_hi[...], v_lo) + dot_nt(h_lo[...], v_hi))
    out[:, pl.ds(first, count)] = -jnp.log(1.0 - v)


def sirt_kernel(
    dims,
    starts,
    offs,
    cs,
    image,
    table_in,
    volume,
    res,
    rec,
    x0,
    img,
    ping,
    pong,
    h_hi,
    h_lo,
    parts_hi,
    parts_lo,
    pick,
    copy_out,
    copy_sum,
    sums,
    w_hi,
    w_lo,
    xb,
    pad,
    xg,
    xh,
    zs0,
    zr0,
    zs1,
    zr1,
    dg,
    dh,
    dr,
    tile,
    th,
    pv0,
    pr0,
    pv1,
    pr1,
    ymid,
    yt,
    weight,
    zsum,
    zrsum,
    s_sum,
    r_sum,
    s_mid,
    r_mid,
    s_left,
    r_left,
    s_right,
    r_right,
    s_x,
    r_x,
    s_z,
    r_z,
    s_loc,
):
    ns, nz, nx = dims
    slots = 4
    np_group = slots * nx
    na = ns * nz
    quads = ns // 4
    right0 = MID0 + MID
    rightn = BAND - right0
    slab = lax.axis_index("slab")
    ray = lax.axis_index("ray")
    z = ray // nx
    x = lax.rem(ray, nx)

    def at_slab(t):
        return {"slab": lax.rem(slab + t, ns), "ray": ray}

    def at_z(t):
        return {"slab": slab, "ray": lax.rem(z + t, nz) * nx + x}

    def at_x(t):
        return {"slab": slab, "ray": z * nx + lax.rem(x + t, nx)}

    loads = [
        pltpu.make_async_copy(image, img, s_loc.at[7]),
    ]
    x_loads = [
        pltpu.make_async_copy(volume.at[:, s, :], x0.at[:, pl.ds(s * 256, 256)], s_loc.at[s])
        for s in range(slots)
    ]
    for c in x_loads + loads:
        c.start()
    barrier = pltpu.get_barrier_semaphore()
    for t in range(1, nx):
        pl.semaphore_signal(barrier, inc=1, device_id=at_x(t), device_id_type=MESH)
    for t in range(1, nz):
        pl.semaphore_signal(barrier, inc=1, device_id=at_z(t), device_id_type=MESH)
    for t in range(1, ns):
        pl.semaphore_signal(barrier, inc=1, device_id=at_slab(t), device_id_type=MESH)
    pl.semaphore_wait(barrier, nx + nz + ns - 3)

    def send(src, dst, ssem, rsem, device):
        return pltpu.make_async_remote_copy(
            src_ref=src, dst_ref=dst, send_sem=ssem, recv_sem=rsem, device_id=device, device_id_type=MESH
        )

    for c in x_loads:
        c.wait()
    x_out = [
        send(x0, xg.at[x], s_x.at[0, t - 1], r_x.at[0, t - 1], at_x(t)) for t in range(1, nx)
    ]
    for c in x_out:
        c.start()
    y_mid, y_side = [], []
    own_rows = pl.ds(pl.multiple_of(slab * 32, 32), 32)
    for t in range(1, ns):
        to = pl.ds(pl.multiple_of(lax.rem(slab + t, ns) * 32, 32), 32)
        y_mid.append(
            send(
                img.at[to, pl.ds(MID0, MID)], ymid.at[slab], s_mid.at[t - 1], r_mid.at[t - 1], at_slab(t)
            )
        )
        y_side.append(
            send(
                img.at[to, pl.ds(0, MID0)],
                res.at[slab, :, pl.ds(0, MID0)],
                s_left.at[t - 1],
                r_left.at[t - 1],
                at_slab(t),
            )
        )
        y_side.append(
            send(
                img.at[to, pl.ds(right0, rightn)],
                res.at[slab, :, pl.ds(right0, rightn)],
                s_right.at[t - 1],
                r_right.at[t - 1],
                at_slab(t),
            )
        )

    height = img.shape[0]
    h_hi[...], h_lo[...] = split(table_in[0:height, :])
    table = table_in.at[pl.ds(height, 16), :]

    vox = lax.broadcasted_iota(jnp.int32, (1, 256), 1)
    dx = (vox // 16).astype(F32) - 7.5
    dy = lax.rem(vox, 16).astype(F32) - 7.5
    lane_ray = lax.broadcasted_iota(jnp.int32, (TR, 256), 0).astype(F32)

    @pl.loop(0, na)
    def _(a):
        base = lane_ray - (dx * cs[0, a] + dy * cs[8, a])
        rows = pl.ds(pl.multiple_of(a * TR, TR), TR)

        @pl.loop(0, np_group)
        def _(p):
            hat = jnp.maximum(0.0, 1.0 - jnp.abs(base + offs[p, a]))
            hi, lo = split(hat)
            w_hi[p, rows, :] = hi
            w_lo[p, rows, :] = lo

    @pl.loop(0, ns)
    def _(a):
        for p in range(np_group):
            pad[a, pl.ds(p * STRIDE // 8, LEAD // 8)] = jnp.zeros((LEAD // 8, 8, 128), F32)
        pad[a, pl.ds(np_group * STRIDE // 8, LEAD // 8)] = jnp.zeros((LEAD // 8, 8, 128), F32)

    @pl.loop(0, np_group)
    def _(p):
        xb[p, 64:96, :] = jnp.ones((32, 256), BF16)
        xb[p, 96:128, :] = jnp.zeros((32, 256), BF16)

    lane = lax.broadcasted_iota(jnp.int32, (1, 128), 1) // 32

    def one_hot(shape, test):
        r = lax.broadcasted_iota(jnp.int32, shape, 0)
        c = lax.broadcasted_iota(jnp.int32, shape, 1)
        return jnp.where(test(r, c), 1.0, 0.0).astype(BF16)

    for g in range(quads):
        pick[g, :, 0:128] = one_hot(
            (512, 128), lambda r, c: (r % 128 < 64) & (r % 32 == c % 32) & (r // 128 == c // 32)
        )
        pick[g, :, 128:256] = one_hot(
            (512, 128), lambda r, c, g=g: (r % 128 == 64) & (g * 4 + r // 128 == c)
        )
        copy_sum[g] = one_hot((16, 128), lambda r, c, g=g: r == g * 4 + c // 32)
    copy_out[...] = one_hot((128, 512), lambda r, c: (r // 32 == c // 128) & (r % 32 == c % 32))

    def load_shard(source, q, copies):
        for s in range(slots):
            hi, lo = split(source[q, :, pl.ds(s * 256, 256)])
            for k in range(copies):
                xb[q * slots + s, k * 32 : (k + 1) * 32, :] = hi
                low = (k + copies) * 32
                xb[q * slots + s, low : low + 32, :] = lo

    def ahead(t):
        return 2 - t + 3 * (t // 2) + 2 * (t // 3)

    def behind(t):
        return t + t // 2 - 2 * (t // 3)

    def forward(zs, zr, phase):
        with_sums = phase == 0

        @pl.loop(0, nz)
        def _(t):
            o = lax.rem(z + ahead(t), nz)
            rows = pl.ds(pl.multiple_of(o * (ns * TR), ns * TR), ns * TR)

            def weigh(p):
                wide = xb[p, 0:128] if with_sums else xb[p]
                part = dot_nt(w_hi[p, rows, :], wide) + dot_nt(w_lo[p, rows, :], wide)
                if not with_sums:
                    part = part[:, :128] + part[:, 128:]
                at = pl.ds(p * (STRIDE // 8) + LEAD // 8, TR // 8)
                for a in range(ns):
                    pad[a, at] = part[a * TR : (a + 1) * TR].reshape(TR // 8, 8, 128)

            def weigh_all():
                @pl.loop(0, np_group, unroll=16 if with_sums else 8)
                def _(p):
                    weigh(p)

            if phase == 0:
                weigh_all()
            else:
                pl.when(t > 0)(weigh_all)

                @pl.when(t == 0)
                def _():
                    @pl.loop(0, nx)
                    def _(u):
                        off = behind(u)
                        q = lax.rem(x + nx - off, nx)

                        @pl.when(u > 0)
                        def _():
                            part = xh.at[q]
                            send(part, part, s_x.at[2, off - 1], r_x.at[2, off - 1], at_x(1)).wait_recv()

                        load_shard(xh, q, 4)
                        for s in range(slots):
                            weigh(q * slots + s)

            @pl.loop(0, quads)
            def _(g):
                packed = jnp.zeros((RAYS, 128), F32)
                for i in range(4):
                    a = g * 4 + i
                    acc = jnp.zeros((RAYS, 128), F32)
                    for p in range(np_group):
                        first = (p * STRIDE + LEAD) // 8 - starts[p, o * ns + a]
                        acc = acc + pad[a, pl.ds(first, RAYS // 8)].reshape(RAYS, 128)
                    if with_sums:
                        hi, lo = split(acc)
                        parts_hi[0:RAYS, i * 128 : (i + 1) * 128] = hi
                        parts_lo[0:RAYS, i * 128 : (i + 1) * 128] = lo
                    else:
                        packed = jnp.where(lane == i, acc, packed)
                if with_sums:
                    part = dot(parts_hi[0:RAYS], pick[g]) + dot(parts_lo[0:RAYS], pick[g])
                    zs[t, g] = part[:, :128]
                    sums[...] = jnp.where(g == 0, part[:, 128:], part[:, 128:] + sums[...])
                else:
                    zs[t, g] = packed

            if with_sums:
                zsum[t, :, 0:128] = jnp.transpose(sums[0:128])[0:ns]
                zsum[t, :, 128:RAYS] = jnp.transpose(sums[128:RAYS])[0:ns]
                zsum[t, :, RAYS:256] = jnp.ones((ns, 256 - RAYS), F32)

            @pl.when(t < nz - 1)
            def _():
                send(zs.at[t], zr.at[t], s_z.at[phase, t], r_z.at[phase, t], at_z(ahead(t))).start()
                if with_sums:
                    send(zsum.at[t], zrsum.at[t], s_sum.at[t], r_sum.at[t], at_z(ahead(t))).start()

    def end_forward(zs, zr, phase):
        for t in range(nz - 1):
            c = send(zs.at[t], zr.at[t], s_z.at[phase, t], r_z.at[phase, t], at_z(1 + t))
            late.append(c)
            c.wait_recv()
            if phase == 0:
                c = send(zsum.at[t], zrsum.at[t], s_sum.at[t], r_sum.at[t], at_z(1 + t))
                late.append(c)
                c.wait_recv()

    late = []

    def total_rays(zs, zr, index):
        v = zs[nz - 1, index]
        for t in range(nz - 1):
            v = v + zr[t, index]
        return v * (1.0 / ROI)

    def spread(buf, phase):
        out = [
            send(buf.at[z], buf.at[z], s_z.at[phase, t - 1], r_z.at[phase, t - 1], at_z(t))
            for t in range(1, nz)
        ]
        for c in out:
            c.start()
        return out

    def backward(buf, pv, pr, phase):
        pv[...] = jnp.zeros_like(pv)

        @pl.loop(0, nz)
        def _(t):
            off = behind(t)
            o = lax.rem(z + nz - off, nz)

            @pl.when(t > 0)
            def _():
                send(buf.at[o], buf.at[o], s_z.at[phase, off - 1], r_z.at[phase, off - 1], at_z(1)).wait_recv()

            for g in range(quads):
                hi, lo = split(buf[o, g])
                wide = dot(hi, copy_out[...]) + dot(lo, copy_out[...])
                for i in range(4):
                    dr[g * 4 + i] = wide[:, i * 128 : (i + 1) * 128].reshape(RAYS // 8, 8, 128)

            rows = pl.ds(pl.multiple_of(o * (ns * TR), ns * TR), ns * TR)

            @pl.loop(0, nx)
            def _(u):
                q = lax.rem(x + ahead(u), nx)
                for g in range(quads):
                    for j in range(4):
                        a = g * 4 + j
                        out = None
                        for s in range(slots):
                            first = starts[q * slots + s, o * ns + a]
                            v = dr[a, pl.ds(first, TR // 8)].reshape(TR, 128)
                            out = v if s == 0 else jnp.where(lane == s, v, out)
                        tile[j * TR : (j + 1) * TR, :] = out
                    hi, lo = split(jnp.transpose(tile[...]))
                    for s in range(slots):
                        th[s, 0:32, g * 128 : (g + 1) * 128] = hi[s * 32 : (s + 1) * 32]
                        th[s, 32:64, g * 128 : (g + 1) * 128] = lo[s * 32 : (s + 1) * 32]
                for s in range(slots):
                    p = q * slots + s
                    both = dot(th[s], w_hi[p, rows, :])
                    low = dot(th[s, 0:32], w_lo[p, rows, :])
                    cols = slice(s * 256, (s + 1) * 256)
                    pv[u, :, cols] = pv[u, :, cols] + (both[:32] + (both[32:] + low))

                @pl.when((t == nz - 1) & (u < nx - 1))
                def _():
                    send(pv.at[u], pr.at[u], s_x.at[phase, u], r_x.at[phase, u], at_x(ahead(u))).start()

        for t in range(nx - 1):
            c = send(pv.at[t], pr.at[t], s_x.at[phase, t], r_x.at[phase, t], at_x(1 + t))
            late.append(c)
            c.wait_recv()
        v = pv[nx - 1]
        for t in range(nx - 1):
            v = v + pr[t]
        return v * (RELAX / (ns * nz * nx))

    for c in loads:
        c.wait()
    modes = filter_forward(img, h_hi, h_lo, table, ping, pong)

    filter_back(modes, h_hi, h_lo, img, MID0, MID)
    for c in y_mid:
        c.start()

    xg[x] = x0[...]
    for c in x_out:
        c.wait()
    for q in range(nx):
        load_shard(xg, q, 1)
    forward(zs0, zr0, 0)

    for base in (0, right0):

        @pl.loop(0, 3)
        def _(i, base=base):
            filter_back(modes, h_hi, h_lo, img, pl.multiple_of(base + i * 256, 128), 256)

        filter_back(modes, h_hi, h_lo, img, base + 768, 128)
    for c in y_side:
        c.start()
    ymid[slab] = img[own_rows, MID0 : MID0 + MID]
    res[slab] = img[own_rows, :]
    for c in y_mid:
        c.wait()
    for g in range(quads):
        block = ymid[g * 4 : (g + 1) * 4].reshape(128, MID)
        for h in range(MID // 128):
            yt[g, h * 128 : (h + 1) * 128, :] = jnp.transpose(block[:, h * 128 : (h + 1) * 128])
    end_forward(zs0, zr0, 0)
    total = zsum[nz - 1]
    for t in range(nz - 1):
        total = total + zrsum[t]
    inverse = 1.0 / jnp.maximum(total * (1.0 / ROI), ROW_FLOOR)
    inv_hi, inv_lo = split(jnp.concatenate([inverse, jnp.zeros_like(inverse)], axis=0))
    for g in range(quads):
        weight[g] = (dot_tn(inv_hi, copy_sum[g]) + dot_tn(inv_lo, copy_sum[g]))[:RAYS]
    for g in range(quads):
        dg[z, g] = (yt[g, SKIP : SKIP + RAYS, :] - total_rays(zs0, zr0, g)) * weight[g]
    d_out = spread(dg, 1)
    first = x0[...] + backward(dg, pv0, pr0, 1)
    late.extend(d_out)
    xh[x] = first
    x_out = [
        send(xh.at[x], xh.at[x], s_x.at[2, t - 1], r_x.at[2, t - 1], at_x(t)) for t in range(1, nx)
    ]
    for c in x_out:
        c.start()
    forward(zs1, zr1, 2)
    late.extend(x_out)
    end_forward(zs1, zr1, 2)
    for g in range(quads):
        diff = yt[g, SKIP : SKIP + RAYS, :] - total_rays(zs1, zr1, g)
        dh[z, g] = diff * weight[g]
        yt[g, SKIP : SKIP + RAYS, :] = diff
    d_out = spread(dh, 3)
    for g in range(quads):
        for h in range(MID // 128):
            turned = jnp.transpose(yt[g, h * 128 : (h + 1) * 128, :]).reshape(4, 32, 128)
            res[g * 4 : (g + 1) * 4, :, MID0 + h * 128 : MID0 + (h + 1) * 128] = turned
    last = first + backward(dh, pv1, pr1, 3)
    for s in range(slots):
        rec[:, s, :] = last[:, s * 256 : (s + 1) * 256]
    late.extend(d_out)

    for c in y_side:
        c.wait()
    for c in late:
        c.wait_send()


def sirt(starts, offs, cs, image, volume, dims):
    height, width = image.shape
    table = filter_tables(height, width)
    anywhere = pl.BlockSpec(memory_space=pl.ANY)
    ns, nz, nx = dims
    np_group = 4 * nx
    na = ns * nz
    rows = na * TR
    quads = ns // 4
    dma = pltpu.SemaphoreType.DMA
    vm = pltpu.VMEM
    smem = pl.BlockSpec(memory_space=pltpu.SMEM)
    peers_z = max(nz - 1, 1)
    peers_x = max(nx - 1, 1)
    return pl.pallas_call(
        functools.partial(sirt_kernel, dims),
        out_shape=(
            jax.ShapeDtypeStruct((ns, 32, BAND), F32),
            jax.ShapeDtypeStruct(volume.shape, F32),
        ),
        in_specs=[smem] * 3 + [anywhere, pl.BlockSpec(memory_space=pltpu.VMEM), anywhere],
        out_specs=(pl.BlockSpec(memory_space=pltpu.VMEM), pl.BlockSpec(memory_space=pltpu.VMEM)),
        scratch_shapes=[
            vm((32, 1024), F32),
            vm((height, width), F32),
            vm((height // 128, width + 2 * HALO, 128), F32),
            vm((height // 128, width + 2 * HALO, 128), F32),
            vm((height, height), BF16),
            vm((height, height), BF16),
            vm((192, 512), BF16),
            vm((192, 512), BF16),
            vm((quads, 512, 256), BF16),
            vm((128, 512), BF16),
            vm((quads, 16, 128), BF16),
            vm((RAYS, 128), F32),
            vm((np_group, rows, 256), BF16),
            vm((np_group, rows, 256), BF16),
            vm((np_group, 256, 256), BF16),
            vm((ns, (np_group * STRIDE + LEAD) // 8, 8, 128), F32),
            vm((nx, 32, 1024), F32),
            vm((nx, 32, 1024), F32),
            vm((nz, quads, RAYS, 128), F32),
            vm((peers_z, quads, RAYS, 128), F32),
            vm((nz, quads, RAYS, 128), F32),
            vm((peers_z, quads, RAYS, 128), F32),
            vm((nz, quads, RAYS, 128), F32),
            vm((nz, quads, RAYS, 128), F32),
            vm((ns, RAYS // 8, 8, 128), F32),
            vm((128, 128), F32),
            vm((4, 64, ns * TR), BF16),
            vm((nx, 32, 1024), F32),
            vm((peers_x, 32, 1024), F32),
            vm((nx, 32, 1024), F32),
            vm((peers_x, 32, 1024), F32),
            vm((ns, 32, MID), F32),
            vm((quads, MID, 128), F32),
            vm((quads, RAYS, 128), F32),
            vm((nz, ns, 256), F32),
            vm((peers_z, ns, 256), F32),
            dma((peers_z,)),
            dma((peers_z,)),
            dma((ns - 1,)),
            dma((ns - 1,)),
            dma((ns - 1,)),
            dma((ns - 1,)),
            dma((ns - 1,)),
            dma((ns - 1,)),
            dma((4, peers_x)),
            dma((4, peers_x)),
            dma((4, peers_z)),
            dma((4, peers_z)),
            dma((8,)),
        ],
        compiler_params=pltpu.CompilerParams(
            collective_id=0, has_side_effects=True, vmem_limit_bytes=51 << 20
        ),
        name="sirt",
    )(starts, offs, cs, image, jnp.asarray(table), volume)


def tables_kernel(dims, angles, ids, starts, offs, cs):
    ns, nz, nx = dims
    ray = lax.axis_index("ray")
    z = ray // nx
    x = lax.rem(ray, nx)
    shape = (4 * nx, 128)
    row = lax.broadcasted_iota(jnp.int32, shape, 0)
    lane = lax.broadcasted_iota(jnp.int32, shape, 1)
    theta = jnp.zeros(shape, F32)
    for a in range(ns * nz):
        theta = jnp.where(lane == a, angles[a % ns, a // ns * nx + x], theta)
    patch = jnp.zeros(shape, jnp.int32)
    for p in range(4 * nx):
        patch = jnp.where(row == p, ids[z * 4 * nx + p], patch)
    cosine = jnp.cos(theta)
    sine = jnp.sin(theta)
    centre_x = (patch // PGRID).astype(F32) * 16.0 + 7.5 - HALF_ROI
    centre_y = (patch % PGRID).astype(F32) * 16.0 + 7.5 - HALF_ROI
    centre = HALF_BAND + centre_x * cosine + centre_y * sine
    first = jnp.floor(centre - 11.61).astype(jnp.int32) + 1
    start = jnp.minimum((first - RAY0) // 8, (RAYS - TR) // 8)
    starts[...] = start
    offs[...] = (start * 8 + RAY0).astype(F32) - centre
    cs[0:8, :] = cosine[0:8]
    cs[8:16, :] = sine[0:8]


def tile_tables(angles, vol_list, dims):
    shape = (4 * dims[2], 128)
    return pl.pallas_call(
        functools.partial(tables_kernel, dims),
        out_shape=(
            jax.ShapeDtypeStruct(shape, jnp.int32),
            jax.ShapeDtypeStruct(shape, F32),
            jax.ShapeDtypeStruct((16, 128), F32),
        ),
        in_specs=[pl.BlockSpec(memory_space=pltpu.SMEM)] * 2,
        out_specs=(pl.BlockSpec(memory_space=pltpu.VMEM),) * 3,
        compiler_params=pltpu.CompilerParams(vmem_limit_bytes=4 << 20),
        name="tile_tables",
    )(angles, vol_list)


def local(dims, intensity, angles, volume, vol_list):
    ns, nz, nx = dims
    height = intensity.shape[2]
    starts, offs, cs = tile_tables(angles, vol_list, dims)
    res, rec = sirt(starts, offs, cs, intensity.reshape(height, BAND), volume, dims)
    return rec, res[:, None]


def make(mesh, dims):
    placed = (P("slab", "ray", None, None), P(), P("slab", "ray", None), P())
    return jax.shard_map(
        functools.partial(local, dims),
        mesh=mesh,
        in_specs=placed,
        out_specs=(P("slab", "ray", None), P(None, "ray", "slab", None)),
        check_vma=False,
    )


def solution(mesh):
    return make(mesh, (mesh.shape["slab"], 4, mesh.shape["ray"] // 4))
```
